256 devices in a mesh: row: 16 (over z, y_hi), col: 16 (over x, y_lo, core).
Axes of the slice: x: 4, y: 4 (y_hi: 2, y_lo: 2; y = y_hi * 2 + y_lo), z: 8, core: 2. Of those that a mesh axis runs over, the one named last changes fastest.
Arguments:
- patches: bfloat16 [32, 8, 8, 8192], P('row', None, None, 'col'), may hold values from -6 to 6
- out_grad: bfloat16 [32, 8, 8, 8192], P('row', None, None, 'col'), may hold values from -6 to 6
- conv_kernel: float32 [3, 3, 3, 8192], P(None, None, None, 'col'), may hold values from -1.25 to 1.25
- saved_gate: bfloat16 [2048, 14336], P('col', 'row'), may hold values from -6 to 6
- saved_up: bfloat16 [2048, 14336], P('col', 'row'), may hold values from -6 to 6
- w_gate: bfloat16 [8192, 14336], P('col', 'row'), may hold values from -0.0625 to 0.0625
- w_up: bfloat16 [8192, 14336], P('col', 'row'), may hold values from -0.0625 to 0.0625
- w_down: bfloat16 [14336, 8192], P('row', 'col'), may hold values from -0.046875 to 0.046875
Outputs:
- patch_grad: bfloat16 [32, 8, 8, 8192], P('row', None, None, 'col')
- kernel_grad: float32 [3, 3, 3, 8192], P(None, None, None, 'col')
- gate_wgrad: bfloat16 [8192, 14336], P('col', 'row')
- up_wgrad: bfloat16 [8192, 14336], P('col', 'row')
- down_wgrad: bfloat16 [14336, 8192], P('row', 'col')
The draws below stay inside these ranges and needn't reach their ends.
All inputs are finite; a program needn't handle non-finite values.
Results may differ from the reference program's by a relative error of at most 0.02.
Values may be sent and summed in bfloat16 or wider, within the bound.
A program may use at most 128 MiB of HBM per device.

```python
import jax
import jax.numpy as jnp
from jax import lax

D = 8192
FF = 14336
YD = 8
XD = 8
ZD = 32
TOKENS = 2048
N_ROW = 16
N_COL = 16


def block_levels(stream_key, extent, cuts, least, largest):
    loudness, own = 1.0, jax.random.fold_in(stream_key, 6)
    for axis_at, shards_of in cuts:
        heights = jnp.exp(jax.random.uniform(jax.random.fold_in(own, axis_at), (shards_of,), jnp.float32, least / len(cuts), largest / len(cuts)))
        loudness = loudness * jnp.repeat(heights, extent[axis_at] // shards_of).reshape([-1 if axis == axis_at else 1 for axis in range(len(extent))])
    return loudness


def gaussian(key, extent, scale, bound, pieces=(), dtype=jnp.bfloat16):
    loudness = block_levels(key, extent, pieces, -0.22, 0.18) if pieces else 1.0
    entries = jax.random.normal(key, extent, jnp.float32) * scale * loudness
    return jnp.minimum(jnp.maximum(entries, -bound), bound).astype(dtype)


def setup_inputs(seed: int = 0) -> dict:
    keys = jax.random.split(jax.random.key(seed), 9)
    patches = gaussian(keys[0], (ZD, YD, XD, D), 1.0, 6.0, ((0, 16), (3, 16)))
    out_grad = gaussian(keys[1], (ZD, YD, XD, D), 0.5, 6.0, ((0, 16), (3, 16)))
    conv_kernel = gaussian(keys[2], (3, 3, 3, D), 27 ** -0.5, 1.25, ((3, 16),), jnp.float32)
    saved_gate = gaussian(keys[3], (TOKENS, FF), 1.0, 6.0, ((0, 16), (1, 16)))
    saved_up = gaussian(keys[4], (TOKENS, FF), 1.0, 6.0, ((0, 16), (1, 16)))
    w_gate = gaussian(keys[5], (D, FF), D ** -0.5, 0.0625, ((0, 16), (1, 16)))
    w_up = gaussian(keys[6], (D, FF), D ** -0.5, 0.0625, ((0, 16), (1, 16)))
    w_down = gaussian(keys[7], (FF, D), FF ** -0.5, 0.046875, ((0, 16), (1, 16)))
    return {"patches": patches, "out_grad": out_grad, "conv_kernel": conv_kernel, "saved_gate": saved_gate, "saved_up": saved_up, "w_gate": w_gate, "w_up": w_up, "w_down": w_down}


def correlate(framed, kernel, flipped):
    planes = framed.shape[0] - 2
    height = framed.shape[1] - 2
    breadth = framed.shape[2] - 2
    summed = jnp.zeros((planes, height, breadth, framed.shape[3]), jnp.float32)
    for along_z in range(3):
        for along_y in range(3):
            for along_x in range(3):
                if flipped:
                    lead_z, lead_y, lead_x = 2 - along_z, 2 - along_y, 2 - along_x
                else:
                    lead_z, lead_y, lead_x = along_z, along_y, along_x
                window = framed[lead_z:lead_z + planes, lead_y:lead_y + height, lead_x:lead_x + breadth]
                summed = summed + kernel[along_z, along_y, along_x] * window
    return summed


def frame(field):
    return jnp.pad(field, ((1, 1), (1, 1), (1, 1), (0, 0)))


def tap_sums(grads, framed):
    planes, height, breadth = grads.shape[0], grads.shape[1], grads.shape[2]
    layers = []
    for along_z in range(3):
        for along_y in range(3):
            for along_x in range(3):
                window = framed[along_z:along_z + planes, along_y:along_y + height, along_x:along_x + breadth]
                layers.append(jnp.sum(grads * window, axis=(0, 1, 2)))
    return jnp.stack(layers).reshape(3, 3, 3, grads.shape[3])


def reference(patches, out_grad, conv_kernel, saved_gate, saved_up, w_gate, w_up, w_down):
    patch_f = patches.astype(jnp.float32)
    framed_in = frame(patch_f)
    mixed_in = (patch_f + correlate(framed_in, conv_kernel, False)).astype(jnp.bfloat16)
    flat_in = mixed_in.reshape(TOKENS, D)
    flat_grad = out_grad.reshape(TOKENS, D)
    block_width = D // N_COL
    hidden_grad = jnp.zeros((TOKENS, FF), jnp.float32)
    for block in range(N_COL):
        grad_block = flat_grad[:, block * block_width:(block + 1) * block_width]
        down_block = w_down[:, block * block_width:(block + 1) * block_width]
        partial_value = lax.dot_general(grad_block, down_block, (((1,), (1,)), ((), ())), preferred_element_type=jnp.float32)
        rounded = lax.optimization_barrier(partial_value.astype(jnp.bfloat16))
        hidden_grad = hidden_grad + rounded.astype(jnp.float32)
    gate_f = saved_gate.astype(jnp.float32)
    up_f = saved_up.astype(jnp.float32)
    sigmoid_g = jax.nn.sigmoid(gate_f)
    silu_g = gate_f * sigmoid_g
    hidden_act = (silu_g * up_f).astype(jnp.bfloat16)
    gate_grad = (hidden_grad * up_f * sigmoid_g * (1.0 + gate_f * (1.0 - sigmoid_g))).astype(jnp.bfloat16)
    up_grad = (hidden_grad * silu_g).astype(jnp.bfloat16)
    contract_rows = (((0,), (0,)), ((), ()))
    down_wgrad = lax.dot_general(hidden_act, flat_grad, contract_rows, preferred_element_type=jnp.float32).astype(jnp.bfloat16)
    gate_wgrad = lax.dot_general(flat_in, gate_grad, contract_rows, preferred_element_type=jnp.float32).astype(jnp.bfloat16)
    up_wgrad = lax.dot_general(flat_in, up_grad, contract_rows, preferred_element_type=jnp.float32).astype(jnp.bfloat16)
    contract_cols = (((1,), (1,)), ((), ()))
    unit_width = FF // N_ROW
    total_grad = flat_grad.astype(jnp.float32)
    for block in range(N_ROW):
        lower = block * unit_width
        upper = (block + 1) * unit_width
        term = lax.dot_general(gate_grad[:, lower:upper], w_gate[:, lower:upper], contract_cols, preferred_element_type=jnp.float32)
        term = term + lax.dot_general(up_grad[:, lower:upper], w_up[:, lower:upper], contract_cols, preferred_element_type=jnp.float32)
        rounded = lax.optimization_barrier(term.astype(jnp.bfloat16))
        total_grad = total_grad + rounded.astype(jnp.float32)
    total_grad = total_grad.reshape(ZD, YD, XD, D)
    patch_grad = (total_grad + correlate(frame(total_grad), conv_kernel, True)).astype(jnp.bfloat16)
    kernel_grad = tap_sums(total_grad, framed_in)
    return (patch_grad, kernel_grad, gate_wgrad, up_wgrad, down_wgrad)
```

```python
import functools

import jax
import jax.numpy as jnp
from jax import lax
from jax.experimental import pallas as pl
from jax.experimental.pallas import tpu as pltpu
from jax.sharding import PartitionSpec as P

MESH = pl.DeviceIdType.MESH
BF = jnp.bfloat16
F32 = jnp.float32


class Sends:
    def __init__(self, sems):
        self.sems, self.made = sems, []

    def go(self, src, dst, recv, device):
        copy = pltpu.make_async_remote_copy(
            src_ref=src,
            dst_ref=dst,
            send_sem=self.sems.at[len(self.made)],
            recv_sem=recv,
            device_id=device,
            device_id_type=MESH,
        )
        copy.start()
        self.made.append(copy)

    def finish(self):
        for copy in self.made:
            copy.wait_send()


def arrived(dst, recv, sem, device):
    pltpu.make_async_remote_copy(
        src_ref=dst, dst_ref=dst, send_sem=sem, recv_sem=recv, device_id=device, device_id_type=MESH
    ).wait_recv()


class Place:
    def __init__(self):
        r, c = lax.axis_index("row"), lax.axis_index("col")
        self.r, self.c = r, c
        self.z, self.h = r // 2, r % 2
        self.x, self.l, self.k = c // 4, (c // 2) % 2, c % 2
        self.zp, self.zm = ((r + 2) % 16, c), ((r + 14) % 16, c)
        self.hp = (r + 1 - 2 * self.h, c)
        self.xp, self.xm = (r, (c + 4) % 16), (r, (c + 12) % 16)
        self.lp = (r, c + 2 - 4 * self.l)
        self.kp = (r, c + 1 - 2 * self.k)

    def slab(self, dz, other):
        hh = self.h + other * (1 - 2 * self.h)
        return ((self.z + dz + 8) % 8) * 2 + hh

    def tile(self, dx, other, k=None):
        ll = self.l + other * (1 - 2 * self.l)
        return ((self.x + dx + 4) % 4) * 4 + ll * 2 + (self.k if k is None else k)


def meet(peers):
    barrier = pltpu.get_barrier_semaphore()
    for peer in peers:
        pl.semaphore_signal(barrier, inc=1, device_id=peer, device_id_type=MESH)
    pl.semaphore_wait(barrier, len(peers))


class RowGather:
    def __init__(self, at, sends, buf, recv):
        self.at, self.sends, self.buf, self.recv = at, sends, buf, recv

    def start(self, own):
        at = self.at
        for peer, way in ((at.hp, 0), (at.zp, 0), (at.zm, 1)):
            self.sends.go(own, self.buf.at[at.r], self.recv.at[way, at.r], peer)

    def wait(self, j, way, rows=None):
        ref = self.buf.at[j] if rows is None else self.buf.at[j, pl.ds(rows, 64)]
        arrived(ref, self.recv.at[way, j], self.sends.sems.at[0], self.at.hp)

    def pair(self):
        at = self.at
        j = at.slab(0, 1)
        self.wait(j, 0)
        for peer, way in ((at.zp, 0), (at.zm, 1)):
            self.sends.go(self.buf.at[j], self.buf.at[j], self.recv.at[way, j], peer)
        return [j]

    def step(self, s, other):
        at = self.at
        if s == 4:
            j = at.slab(4, other)
            self.wait(j, 0, 0)
            self.wait(j, 1, 64)
            return [j]
        got = []
        for way, dz, peer in ((0, -s, at.zp), (1, s, at.zm)):
            j = at.slab(dz, other)
            self.wait(j, way)
            ref = self.buf.at[j] if s < 3 else self.buf.at[j, pl.ds(64 * way, 64)]
            self.sends.go(ref, ref, self.recv.at[way, j], peer)
            got.append(j)
        return got


class ColGather:
    def __init__(self, at, sends, buf, recv):
        self.at, self.sends, self.buf, self.recv = at, sends, buf, recv

    def start(self, own):
        at = self.at
        for peer, way in ((at.lp, 0), (at.xp, 0), (at.xm, 1), (at.kp, 0)):
            self.sends.go(own, self.buf.at[at.c], self.recv.at[way, at.c], peer)

    def wait(self, j, way, rows=None):
        ref = self.buf.at[j] if rows is None else self.buf.at[j, pl.ds(rows, 64)]
        arrived(ref, self.recv.at[way, j], self.sends.sems.at[0], self.at.kp)

    def pair(self):
        at = self.at
        j = at.tile(0, 1)
        self.wait(j, 0)
        for peer, way in ((at.xp, 0), (at.xm, 1), (at.kp, 0)):
            self.sends.go(self.buf.at[j], self.buf.at[j], self.recv.at[way, j], peer)

    def step(self, s, other):
        at = self.at
        if s == 2:
            j = at.tile(2, other)
            self.wait(j, 0, 0)
            self.wait(j, 1, 64)
            self.sends.go(self.buf.at[j], self.buf.at[j], self.recv.at[0, j], at.kp)
            return
        for way, dx, peer in ((0, -1, at.xp), (1, 1, at.xm)):
            j = at.tile(dx, other)
            self.wait(j, way)
            ref = self.buf.at[j, pl.ds(64 * way, 64)]
            self.sends.go(ref, ref, self.recv.at[way, j], peer)
            self.sends.go(self.buf.at[j], self.buf.at[j], self.recv.at[0, j], at.kp)

    def rest(self):
        for dx, other in ((0, 0), (0, 1), (1, 0), (1, 1), (-1, 0), (-1, 1), (2, 0), (2, 1)):
            self.wait(self.at.tile(dx, other, 1 - self.at.k), 0)


def front(
    og, xin, gate, up, wd,
    dy_all, x_all, g_all, u_all, dh_all,
    wdt, part, mate, stage, xp_half, xm_half, xp_full, xm_full, y_full,
    send_sem, dy_sem, x_sem, g_sem, u_sem, dh_sem, mate_sem, ring_sem,
):
    at = Place()
    sends = Sends(send_sem)
    meet((at.zp, at.zm, at.hp, at.xp, at.xm, at.lp, at.kp))
    dy = RowGather(at, sends, dy_all, dy_sem)
    xg = RowGather(at, sends, x_all, x_sem)
    gg = ColGather(at, sends, g_all, g_sem)
    ug = ColGather(at, sends, u_all, u_sem)
    dg = ColGather(at, sends, dh_all, dh_sem)
    dy.start(og)
    gg.start(gate)
    ug.start(up)
    dy_all[at.r] = og[...]
    g_all[at.c] = gate[...]
    u_all[at.c] = up[...]
    x_all[at.r] = xin[...]
    wdt[...] = wd[...].T

    def partial(j):
        part[j] = jnp.dot(dy_all[j], wdt[...], preferred_element_type=F32).astype(BF)

    def to_mate(zz):
        j = zz * 2 + 1 - at.k
        sends.go(part.at[j], mate.at[zz], mate_sem.at[zz], at.kp)

    def zed(dz):
        return (at.z + dz + 8) % 8

    partial(at.r)
    for j in dy.pair():
        partial(j)
    to_mate(at.z)
    gg.pair()
    ug.pair()
    for s in (1, 2, 3):
        for other in (0, 1):
            for j in dy.step(s, other):
                partial(j)
            if s == 1:
                gg.step(1, other)
            elif s == 2:
                gg.step(2, other)
            else:
                ug.step(1, other)
        to_mate(zed(s))
        to_mate(zed(-s))
    for other in (0, 1):
        for j in dy.step(4, other):
            partial(j)
    to_mate(zed(4))
    xg.start(xin)
    for other in (0, 1):
        ug.step(2, other)
    xg.pair()

    def summed(xx, ll):
        zz = xx * 2 + ll
        arrived(mate.at[zz], mate_sem.at[zz], send_sem.at[0], at.kp)
        return part[zz * 2 + at.k].astype(F32) + mate[zz].astype(F32)

    def ex(dx):
        return (at.x + dx + 4) % 4

    for ll in (0, 1):
        stage[0, ll] = summed(ex(2), ll).astype(BF)
        sends.go(stage.at[0, ll, pl.ds(0, 64)], xp_half.at[ll], ring_sem.at[0, ll], at.xp)
        sends.go(stage.at[0, ll, pl.ds(64, 64)], xm_half.at[ll], ring_sem.at[1, ll], at.xm)
    for other in (0, 1):
        xg.step(1, other)
    for ll in (0, 1):
        total = summed(ex(1), ll)
        arrived(xp_half.at[ll], ring_sem.at[0, ll], send_sem.at[0], at.xm)
        stage[1, ll, 0:64] = (total[0:64] + xp_half[ll].astype(F32)).astype(BF)
        stage[1, ll, 64:128] = total[64:128].astype(BF)
        sends.go(stage.at[1, ll], xp_full.at[ll], ring_sem.at[2, ll], at.xp)
        total = summed(ex(-1), ll)
        arrived(xm_half.at[ll], ring_sem.at[1, ll], send_sem.at[0], at.xp)
        stage[2, ll, 0:64] = total[0:64].astype(BF)
        stage[2, ll, 64:128] = (total[64:128] + xm_half[ll].astype(F32)).astype(BF)
        sends.go(stage.at[2, ll], xm_full.at[ll], ring_sem.at[3, ll], at.xm)
    for other in (0, 1):
        xg.step(2, other)

    def whole(ll, which):
        total = summed(at.x, ll)
        arrived(xp_full.at[ll], ring_sem.at[2, ll], send_sem.at[0], at.xm)
        arrived(xm_full.at[ll], ring_sem.at[3, ll], send_sem.at[0], at.xp)
        return total + xp_full[ll].astype(F32) + xm_full[ll].astype(F32)

    stage[3, 0] = whole(1 - at.l, 0).astype(BF)
    sends.go(stage.at[3, 0], y_full, ring_sem.at[4, 0], at.lp)
    mine = whole(at.l, 1)
    arrived(y_full, ring_sem.at[4, 0], send_sem.at[0], at.lp)
    dh_all[at.c] = (mine + y_full[...].astype(F32)).astype(BF)
    dg.start(dh_all.at[at.c])
    for other in (0, 1):
        xg.step(3, other)
    dg.pair()
    for other in (0, 1):
        dg.step(1, other)
    for other in (0, 1):
        dg.step(2, other)
    for other in (0, 1):
        xg.step(4, other)
    gg.rest()
    ug.rest()
    dg.rest()
    sends.finish()


def back(og, parts, out, stage, half, full, pair, send_sem, ring_sem):
    at = Place()
    sends = Sends(send_sem)
    meet((at.zp, at.zm, at.hp))
    for other in (0, 1):
        j = at.slab(4, other)
        for way, peer in ((0, at.zp), (1, at.zm)):
            rows = pl.ds(64 * way, 64)
            sends.go(parts.at[j, rows], half.at[way, other], ring_sem.at[0, way, other], peer)
    for t in (1, 2, 3):
        for other in (0, 1):
            for way, peer, source in ((0, at.zp, at.zm), (1, at.zm, at.zp)):
                j = at.slab((4 - t) * (1 - 2 * way), other)
                held = stage.at[t - 1, way, other]
                if t == 1:
                    lo = 64 * way
                    arrived(half.at[way, other], ring_sem.at[0, way, other], send_sem.at[0], source)
                    held[lo : lo + 64] = (
                        parts[j, lo : lo + 64].astype(F32) + half[way, other].astype(F32)
                    ).astype(BF)
                    held[64 - lo : 128 - lo] = parts[j, 64 - lo : 128 - lo]
                else:
                    came = full.at[t - 2, way, other]
                    arrived(came, ring_sem.at[t - 1, way, other], send_sem.at[0], source)
                    held[...] = (parts[j].astype(F32) + came[...].astype(F32)).astype(BF)
                sends.go(held, full.at[t - 1, way, other], ring_sem.at[t, way, other], peer)

    def whole(other):
        j = at.slab(0, other)
        total = parts[j].astype(F32)
        for way, source in ((0, at.zm), (1, at.zp)):
            came = full.at[2, way, other]
            arrived(came, ring_sem.at[3, way, other], send_sem.at[0], source)
            total = total + came[...].astype(F32)
        return total

    pair[0] = whole(1).astype(BF)
    sends.go(pair.at[0], pair.at[1], ring_sem.at[4, 0, 0], at.hp)
    mine = og[...].astype(F32) + whole(0)
    arrived(pair.at[1], ring_sem.at[4, 0, 0], send_sem.at[0], at.hp)
    out[...] = mine + pair[1].astype(F32)
    sends.finish()


VM = pl.BlockSpec(memory_space=pltpu.VMEM)
DMA = pltpu.SemaphoreType.DMA


def run_front(og, xin, gate, up, wd):
    feats, units = og.shape[1], gate.shape[1]
    tok = (16, 128, feats)
    hid = (16, 128, units)
    return pl.pallas_call(
        front,
        out_shape=[jax.ShapeDtypeStruct(s, BF) for s in (tok, tok, hid, hid, hid)],
        in_specs=[VM] * 5,
        out_specs=[VM] * 5,
        scratch_shapes=[
            pltpu.VMEM((feats, units), BF),
            pltpu.VMEM(hid, BF),
            pltpu.VMEM((8, 128, units), BF),
            pltpu.VMEM((4, 2, 128, units), BF),
            pltpu.VMEM((2, 64, units), BF),
            pltpu.VMEM((2, 64, units), BF),
            pltpu.VMEM((2, 128, units), BF),
            pltpu.VMEM((2, 128, units), BF),
            pltpu.VMEM((128, units), BF),
            DMA((120,)),
            DMA((2, 16)),
            DMA((2, 16)),
            DMA((2, 16)),
            DMA((2, 16)),
            DMA((2, 16)),
            DMA((8,)),
            DMA((5, 2)),
        ],
        compiler_params=pltpu.CompilerParams(collective_id=0, has_side_effects=True),
        name="front",
    )(og, xin, gate, up, wd)


def run_back(og, parts):
    feats = og.shape[1]
    return pl.pallas_call(
        back,
        out_shape=jax.ShapeDtypeStruct((128, feats), F32),
        in_specs=[VM] * 2,
        out_specs=VM,
        scratch_shapes=[
            pltpu.VMEM((3, 2, 2, 128, feats), BF),
            pltpu.VMEM((2, 2, 64, feats), BF),
            pltpu.VMEM((3, 2, 2, 128, feats), BF),
            pltpu.VMEM((2, 128, feats), BF),
            DMA((20,)),
            DMA((5, 2, 2)),
        ],
        compiler_params=pltpu.CompilerParams(collective_id=1, has_side_effects=True),
        name="back",
    )(og, parts)


def padded(x, sides, width):
    for axis, dim in sides:
        peers, length = (lax.axis_size(axis), x.shape[dim])
        up = [(i, (i + 1) % peers) for i in range(peers - 1)]
        down = [(j, i) for i, j in up]
        last = lax.slice_in_dim(x, length - width, length, axis=dim)
        first = lax.slice_in_dim(x, 0, width, axis=dim)
        before = lax.ppermute(last, axis, up)
        after = lax.ppermute(first, axis, down)
        x = jnp.concatenate([before, x, after], axis=dim)
    return x


def from_everyone(x, axis):
    peers = lax.axis_size(axis)
    return lax.all_to_all(jnp.broadcast_to(x[None], (peers, *x.shape)), axis, 0, 0, tiled=True)


def of_everyone(x, axis):
    everything = from_everyone(x, axis)
    return jnp.sum(everything.astype(jnp.float32), axis=0)


def correlate(framed, kernel, flipped):
    planes = framed.shape[0] - 2
    height = framed.shape[1] - 2
    breadth = framed.shape[2] - 2
    summed = jnp.zeros((planes, height, breadth, framed.shape[3]), jnp.float32)
    for along_z in range(3):
        for along_y in range(3):
            for along_x in range(3):
                if flipped:
                    lead_z, lead_y, lead_x = (2 - along_z, 2 - along_y, 2 - along_x)
                else:
                    lead_z, lead_y, lead_x = (along_z, along_y, along_x)
                window = framed[
                    lead_z : lead_z + planes, lead_y : lead_y + height, lead_x : lead_x + breadth
                ]
                summed = summed + kernel[along_z, along_y, along_x] * window
    return summed


def frame_sides(field):
    return jnp.pad(field, ((0, 0), (1, 1), (1, 1), (0, 0)))


def tap_sums(grads, framed):
    planes, height, breadth = (grads.shape[0], grads.shape[1], grads.shape[2])
    layers = []
    for along_z in range(3):
        for along_y in range(3):
            for along_x in range(3):
                window = framed[
                    along_z : along_z + planes,
                    along_y : along_y + height,
                    along_x : along_x + breadth,
                ]
                layers.append(jnp.sum(grads * window, axis=(0, 1, 2)))
    return jnp.stack(layers).reshape(3, 3, 3, grads.shape[3])


def swiglu_back(hidden_grad, gate_in, up_in):
    gate_f = gate_in.astype(jnp.float32)
    up_f = up_in.astype(jnp.float32)
    sigmoid_g = jax.nn.sigmoid(gate_f)
    silu_g = gate_f * sigmoid_g
    hidden_act = (silu_g * up_f).astype(jnp.bfloat16)
    gate_grad = (hidden_grad * up_f * sigmoid_g * (1.0 + gate_f * (1.0 - sigmoid_g))).astype(
        jnp.bfloat16
    )
    up_grad = (hidden_grad * silu_g).astype(jnp.bfloat16)
    return (hidden_act, gate_grad, up_grad)


def body(patches, out_grad, conv_kernel, saved_gate, saved_up, w_gate, w_up, w_down):
    planes, height, breadth, features = patches.shape
    rimmed = padded(patches, (("row", 0),), 1)
    framed_in = frame_sides(rimmed.astype(jnp.float32))
    mixed_in = (patches.astype(jnp.float32) + correlate(framed_in, conv_kernel, False)).astype(
        jnp.bfloat16
    )
    own = planes * height * breadth
    og = out_grad.reshape(own, features)
    flat_grad, flat_in, gate_all, up_all, hidden_grad = (
        a.reshape(16 * own, a.shape[2])
        for a in run_front(og, mixed_in.reshape(own, features), saved_gate, saved_up, w_down)
    )
    contract_cols = (((1,), (1,)), ((), ()))
    contract_rows = (((0,), (0,)), ((), ()))
    hidden_all, gate_grad_all, up_grad_all = swiglu_back(
        hidden_grad.astype(jnp.float32), gate_all, up_all
    )
    term = lax.dot_general(gate_grad_all, w_gate, contract_cols, preferred_element_type=jnp.float32)
    term = term + lax.dot_general(
        up_grad_all, w_up, contract_cols, preferred_element_type=jnp.float32
    )
    total_grad = run_back(og, term.astype(jnp.bfloat16).reshape(16, own, features)).reshape(
        planes, height, breadth, features
    )
    down_wgrad = lax.dot_general(
        hidden_all, flat_grad, contract_rows, preferred_element_type=jnp.float32
    ).astype(jnp.bfloat16)
    gate_wgrad = lax.dot_general(
        flat_in, gate_grad_all, contract_rows, preferred_element_type=jnp.float32
    ).astype(jnp.bfloat16)
    up_wgrad = lax.dot_general(
        flat_in, up_grad_all, contract_rows, preferred_element_type=jnp.float32
    ).astype(jnp.bfloat16)
    grad_rimmed = padded(total_grad.astype(jnp.bfloat16), (("row", 0),), 1).astype(total_grad.dtype)
    patch_grad = (total_grad + correlate(frame_sides(grad_rimmed), conv_kernel, True)).astype(
        jnp.bfloat16
    )
    kernel_grad = of_everyone(tap_sums(total_grad, framed_in).astype(jnp.bfloat16), "row").astype(
        jnp.float32
    )
    return (patch_grad, kernel_grad, gate_wgrad, up_wgrad, down_wgrad)


def solution(mesh):
    return jax.shard_map(
        body,
        mesh=mesh,
        in_specs=(
            P("row", None, None, "col"),
            P("row", None, None, "col"),
            P(None, None, None, "col"),
            P("col", "row"),
            P("col", "row"),
            P("col", "row"),
            P("col", "row"),
            P("row", "col"),
        ),
        out_specs=(
            P("row", None, None, "col"),
            P(None, None, None, "col"),
            P("col", "row"),
            P("col", "row"),
            P("row", "col"),
        ),
        check_vma=False,
    )
```

```python
import jax
import jax.numpy as jnp
from jax import lax
from jax.experimental import pallas as pl
from jax.experimental.pallas import tpu as pltpu
from jax.sharding import PartitionSpec as P

MESH = pl.DeviceIdType.MESH
BF = jnp.bfloat16
F32 = jnp.float32
DMA = pltpu.SemaphoreType.DMA


class Sends:
    def __init__(self, sems):
        self.sems, self.made = sems, []

    def go(self, src, dst, recv, device):
        copy = pltpu.make_async_remote_copy(
            src_ref=src,
            dst_ref=dst,
            send_sem=self.sems.at[len(self.made)],
            recv_sem=recv,
            device_id=device,
            device_id_type=MESH,
        )
        copy.start()
        self.made.append(copy)

    def finish(self):
        for copy in self.made:
            copy.wait_send()

    def arrived(self, dst, recv, device):
        pltpu.make_async_remote_copy(
            src_ref=dst,
            dst_ref=dst,
            send_sem=self.sems.at[0],
            recv_sem=recv,
            device_id=device,
            device_id_type=MESH,
        ).wait_recv()


class Place:
    def __init__(self):
        r, c = lax.axis_index("row"), lax.axis_index("col")
        self.r, self.c = r, c
        self.z, self.h = r // 2, r % 2
        self.x, self.l, self.k = c // 4, (c // 2) % 2, c % 2
        self.zp, self.zm = ((r + 2) % 16, c), ((r + 14) % 16, c)
        self.hp = (r + 1 - 2 * self.h, c)
        self.after, self.before = ((r + 1) % 16, c), ((r + 15) % 16, c)
        self.xp, self.xm = (r, (c + 4) % 16), (r, (c + 12) % 16)
        self.lp = (r, c + 2 - 4 * self.l)
        self.kp = (r, c + 1 - 2 * self.k)

    def slab(self, dz, other):
        hh = self.h + other * (1 - 2 * self.h)
        return ((self.z + dz + 8) % 8) * 2 + hh

    def tile(self, dx, other, k=None):
        ll = self.l + other * (1 - 2 * self.l)
        return ((self.x + dx + 4) % 4) * 4 + ll * 2 + (self.k if k is None else k)


class RowGather:
    def __init__(self, at, sends, buf, recv):
        self.at, self.sends, self.buf, self.recv = at, sends, buf, recv

    def start(self, own):
        at = self.at
        for peer, way in ((at.hp, 0), (at.zp, 0), (at.zm, 1)):
            self.sends.go(own, self.buf.at[at.r], self.recv.at[way, at.r], peer)

    def wait(self, j, way, rows=None):
        ref = self.buf.at[j] if rows is None else self.buf.at[j, pl.ds(rows, 64)]
        self.sends.arrived(ref, self.recv.at[way, j], self.at.hp)

    def pair(self):
        at = self.at
        j = at.slab(0, 1)
        self.wait(j, 0)
        for peer, way in ((at.zp, 0), (at.zm, 1)):
            self.sends.go(self.buf.at[j], self.buf.at[j], self.recv.at[way, j], peer)
        return [j]

    def step(self, s, other):
        at = self.at
        if s == 4:
            j = at.slab(4, other)
            self.wait(j, 0, 0)
            self.wait(j, 1, 64)
            return [j]
        got = []
        for way, dz, peer in ((0, -s, at.zp), (1, s, at.zm)):
            j = at.slab(dz, other)
            self.wait(j, way)
            ref = self.buf.at[j] if s < 3 else self.buf.at[j, pl.ds(64 * way, 64)]
            self.sends.go(ref, ref, self.recv.at[way, j], peer)
            got.append(j)
        return got


class ColGather:
    def __init__(self, at, sends, buf, recv):
        self.at, self.sends, self.buf, self.recv = at, sends, buf, recv

    def start(self, own):
        at = self.at
        for peer, way in ((at.lp, 0), (at.xp, 0), (at.xm, 1), (at.kp, 0)):
            self.sends.go(own, self.buf.at[at.c], self.recv.at[way, at.c], peer)

    def wait(self, j, way, rows=None):
        ref = self.buf.at[j] if rows is None else self.buf.at[j, pl.ds(rows, 64)]
        self.sends.arrived(ref, self.recv.at[way, j], self.at.kp)

    def pair(self):
        at = self.at
        j = at.tile(0, 1)
        self.wait(j, 0)
        for peer, way in ((at.xp, 0), (at.xm, 1), (at.kp, 0)):
            self.sends.go(self.buf.at[j], self.buf.at[j], self.recv.at[way, j], peer)

    def step(self, s, other):
        at = self.at
        if s == 2:
            j = at.tile(2, other)
            self.wait(j, 0, 0)
            self.wait(j, 1, 64)
            self.sends.go(self.buf.at[j], self.buf.at[j], self.recv.at[0, j], at.kp)
            return
        for way, dx, peer in ((0, -1, at.xp), (1, 1, at.xm)):
            j = at.tile(dx, other)
            self.wait(j, way)
            ref = self.buf.at[j, pl.ds(64 * way, 64)]
            self.sends.go(ref, ref, self.recv.at[way, j], peer)
            self.sends.go(self.buf.at[j], self.buf.at[j], self.recv.at[0, j], at.kp)

    def rest(self):
        for dx, other in ((0, 0), (0, 1), (1, 0), (1, 1), (-1, 0), (-1, 1), (2, 0), (2, 1)):
            self.wait(self.at.tile(dx, other, 1 - self.at.k), 0)


def shifts(line):
    at = lax.broadcasted_iota(jnp.int32, line.shape, 0)
    zero = jnp.zeros_like(line)
    return (
        jnp.where(at == 0, zero, pltpu.roll(line, 1, 0)),
        line,
        jnp.where(at == 7, zero, pltpu.roll(line, 7, 0)),
    )


def clear_rim(frame):
    zero = jnp.zeros(frame.shape[3:], F32)
    for e in range(3):
        for plane in range(4):
            frame[e, plane, 0] = zero
            frame[e, plane, 9] = zero


def fill_plane(frame, plane, read):
    def two(i, carry):
        rows = read(i)
        for half in range(2):
            for e, line in enumerate(shifts(rows[8 * half : 8 * half + 8])):
                frame[e, plane, 2 * i + half + 1] = line
        return carry

    lax.fori_loop(0, 4, two, 0)


def convolve(frame, taps, flipped, base, write):
    def line(i, carry):
        for half in range(2):
            y = 2 * i + half
            plane, y = y // 8, y % 8
            total = frame[1, plane + 1, y + 1]
            for a in range(3):
                for b in range(3):
                    for e in range(3):
                        tap = taps[2 - a, 2 - b, 2 - e] if flipped else taps[a, b, e]
                        total = total + tap * frame[e, plane + a, y + b]
            base[8 * half : 8 * half + 8] = total
        write(i, base[...])
        return carry

    lax.fori_loop(0, 8, line, 0)


def tap_totals(grads, frame, store):
    for lanes in range(0, grads.shape[1], 128):
        cut = pl.ds(lanes, 128)

        def line(i, totals):
            plane, y = i // 8, i % 8
            grad = grads[pl.ds(pl.multiple_of(i * 8, 8), 8), cut]
            return tuple(
                totals[9 * a + 3 * b + e] + grad * frame[e, plane + a, y + b, :, cut]
                for a in range(3)
                for b in range(3)
                for e in range(3)
            )

        totals = lax.fori_loop(0, 16, line, tuple(jnp.zeros((8, 128), F32) for _ in range(27)))
        for n, total in enumerate(totals):
            store(n, cut, jnp.sum(total, axis=0, keepdims=True))


def rowwise(n, work):
    def some(i, carry):
        work(pl.ds(pl.multiple_of(i * 32, 32), 32))
        return carry

    lax.fori_loop(0, n // 32, some, 0)


def flat(value):
    return value.reshape(value.shape[0] * value.shape[1], value.shape[2])


def rows_dot(a, b):
    return lax.dot_general(a, b, (((0,), (0,)), ((), ())), preferred_element_type=F32)


def whole(
    px, og, taps, gate, up, wg, wu, wd,
    pgrad, kgrad, gw, uw, dw,
    dy_all, x_all, g_all, u_all, dh_all, hid, ga, ub,
    wdt, wgt, wut, part, mate, stage, xp_half, xm_half, xp_full, xm_full, y_full,
    rstage, rhalf, rfull, rpair,
    px_rim, gr_rim, gr_out, frame, gframe, lines, total, tap_out, tap_in, tap_all,
    send_sem, dy_sem, x_sem, g_sem, u_sem, dh_sem, mate_sem, ring_sem, rring_sem, rim_sem, tap_sem,
):
    at = Place()
    sends = Sends(send_sem)
    barrier = pltpu.get_barrier_semaphore()
    row_peers = [((at.r + d) % 16, at.c) for d in range(1, 16)]
    peers = row_peers + [at.xp, at.xm, at.lp, at.kp]
    for peer in peers:
        pl.semaphore_signal(barrier, inc=1, device_id=peer, device_id_type=MESH)
    wdt[...] = wd[...].T
    dy_all[at.r] = og[...]
    g_all[at.c] = gate[...]
    u_all[at.c] = up[...]
    pl.semaphore_wait(barrier, len(peers))

    dy = RowGather(at, sends, dy_all, dy_sem)
    xg = RowGather(at, sends, x_all, x_sem)
    gg = ColGather(at, sends, g_all, g_sem)
    ug = ColGather(at, sends, u_all, u_sem)
    dg = ColGather(at, sends, dh_all, dh_sem)
    dy.start(og)
    sends.go(px.at[pl.ds(64, 64)], px_rim.at[0], rim_sem.at[0], at.after)
    sends.go(px.at[pl.ds(0, 64)], px_rim.at[1], rim_sem.at[1], at.before)
    gg.start(gate)
    ug.start(up)

    def partial(j):
        part[j] = jnp.dot(dy_all[j], wdt[...], preferred_element_type=F32).astype(BF)

    def to_mate(zz):
        j = zz * 2 + 1 - at.k
        sends.go(part.at[j], mate.at[zz], mate_sem.at[zz], at.kp)

    def zed(dz):
        return (at.z + dz + 8) % 8

    def rims(rim, sem, inside):
        for side, (peer, end) in enumerate(((at.before, 0), (at.after, 15))):
            sends.arrived(rim.at[side], sem.at[side], peer)
            fill_plane(
                inside,
                3 * side,
                lambda i: jnp.where(
                    at.r == end, 0.0, rim[side, pl.ds(pl.multiple_of(i * 16, 16), 16)].astype(F32)
                ),
            )

    partial(at.r)
    clear_rim(frame)
    clear_rim(gframe)
    for plane in (0, 1):
        fill_plane(
            frame,
            plane + 1,
            lambda i: px[pl.ds(pl.multiple_of(plane * 64 + i * 16, 16), 16)].astype(F32),
        )
    for j in dy.pair():
        partial(j)
    to_mate(at.z)
    gg.pair()
    ug.pair()
    for s in (1, 2, 3):
        for other in (0, 1):
            for j in dy.step(s, other):
                partial(j)
            if s == 1:
                gg.step(1, other)
            elif s == 2:
                gg.step(2, other)
            else:
                ug.step(1, other)
        to_mate(zed(s))
        to_mate(zed(-s))
        if s == 1:
            rims(px_rim, rim_sem, frame)

            def mixed(i, value):
                x_all[at.r, pl.ds(pl.multiple_of(i * 16, 16), 16)] = value.astype(BF)

            convolve(frame, taps, False, lines, mixed)
    xg.start(x_all.at[at.r])
    for other in (0, 1):
        for j in dy.step(4, other):
            partial(j)
    to_mate(zed(4))
    for other in (0, 1):
        ug.step(2, other)
    xg.pair()

    def ell(other):
        return at.l + other * (1 - 2 * at.l)

    def summed(xx, ll, rows):
        zz = xx * 2 + ll
        return part[zz * 2 + at.k, rows].astype(F32) + mate[zz, rows].astype(F32)

    def from_mate(xx, ll):
        zz = xx * 2 + ll
        sends.arrived(mate.at[zz], mate_sem.at[zz], at.kp)

    def ex(dx):
        return (at.x + dx + 4) % 4

    for o in (1, 0):
        ll, xx = ell(o), ex(2)
        from_mate(xx, ll)

        def far(rows):
            stage[0, o, rows] = summed(xx, ll, rows).astype(BF)

        rowwise(128, far)
        sends.go(stage.at[0, o, pl.ds(0, 64)], xp_half.at[ll], ring_sem.at[0, ll], at.xp)
        sends.go(stage.at[0, o, pl.ds(64, 64)], xm_half.at[ll], ring_sem.at[1, ll], at.xm)
    for other in (0, 1):
        xg.step(1, other)
    gg.rest()
    ug.rest()

    def swiglu(j):
        def work(rows):
            g, u = g_all[j, rows].astype(F32), u_all[j, rows].astype(F32)
            s = 1.0 / (1.0 + jnp.exp(-g))
            silu = g * s
            hid[j, rows] = (silu * u).astype(BF)
            ga[j, rows] = (u * (s + silu * (1.0 - s))).astype(BF)
            ub[j, rows] = silu.astype(BF)

        rowwise(128, work)

    def swiglus(lo, hi):
        lax.fori_loop(lo, hi, lambda j, carry: (swiglu(j), carry)[1], 0)

    swiglus(0, 4)
    for o in (1, 0):
        ll = ell(o)
        for way, half, full, peer, source in (
            (0, xp_half, xp_full, at.xp, at.xm),
            (1, xm_half, xm_full, at.xm, at.xp),
        ):
            xx = ex(1 - 2 * way)
            from_mate(xx, ll)
            sends.arrived(half.at[ll], ring_sem.at[way, ll], source)

            def near(i, carry):
                rows = pl.ds(pl.multiple_of(64 * way + i * 32, 32), 32)
                came = half[ll, pl.ds(pl.multiple_of(i * 32, 32), 32)].astype(F32)
                stage[1 + way, o, rows] = (summed(xx, ll, rows) + came).astype(BF)
                rows = pl.ds(pl.multiple_of(64 - 64 * way + i * 32, 32), 32)
                stage[1 + way, o, rows] = summed(xx, ll, rows).astype(BF)
                return carry

            lax.fori_loop(0, 2, near, 0)
            sends.go(stage.at[1 + way, o], full.at[ll], ring_sem.at[2 + way, ll], peer)
    swiglus(4, 10)
    for other in (0, 1):
        xg.step(2, other)

    for o in (1, 0):
        ll = ell(o)
        from_mate(at.x, ll)
        sends.arrived(xp_full.at[ll], ring_sem.at[2, ll], at.xm)
        sends.arrived(xm_full.at[ll], ring_sem.at[3, ll], at.xp)
        if o == 0:
            sends.arrived(y_full, ring_sem.at[4, 0], at.lp)

        def last(rows):
            value = summed(at.x, ll, rows) + xp_full[ll, rows].astype(F32)
            value = value + xm_full[ll, rows].astype(F32)
            if o == 1:
                stage[3, 0, rows] = value.astype(BF)
            else:
                dh_all[at.c, rows] = (value + y_full[rows].astype(F32)).astype(BF)

        rowwise(128, last)
        if o == 1:
            sends.go(stage.at[3, 0], y_full, ring_sem.at[4, 0], at.lp)
    dg.start(dh_all.at[at.c])
    swiglus(10, 16)
    dg.pair()
    for other in (0, 1):
        xg.step(3, other)

    def down(lo, n):
        lhs = flat(hid[:, :, lo : lo + n])
        dw[lo : lo + n, :] = rows_dot(lhs, flat(dy_all[...])).astype(BF)

    down(0, 256)
    for other in (0, 1):
        dg.step(1, other)
    wgt[...] = wg[...].T
    wut[...] = wu[...].T
    down(256, 256)
    for other in (0, 1):
        xg.step(4, other)
    for other in (0, 1):
        dg.step(2, other)
    dg.rest()

    def hidden_grads(j):
        def work(rows):
            grad = dh_all[j, rows].astype(F32)
            ga[j, rows] = (ga[j, rows].astype(F32) * grad).astype(BF)
            ub[j, rows] = (ub[j, rows].astype(F32) * grad).astype(BF)

        rowwise(128, work)

    def back(j):
        return jnp.dot(ga[j], wgt[...], preferred_element_type=F32) + jnp.dot(
            ub[j], wut[...], preferred_element_type=F32
        )

    for other in (1, 0):
        j = at.slab(4, other)
        hidden_grads(j)
        total[...] = back(j)
        for way, peer in ((0, at.zp), (1, at.zm)):
            rows = pl.ds(64 * way, 64)
            rstage[0, way, other, rows] = total[rows].astype(BF)
            sends.go(
                rstage.at[0, way, other, rows],
                rhalf.at[way, other],
                rring_sem.at[0, way, other],
                peer,
            )

    def rest_of_hidden(n, carry):
        hidden_grads((at.z * 2 + 10 + n) % 16)
        return carry

    lax.fori_loop(0, 14, rest_of_hidden, 0)

    def wgrad(out, right, lo):
        out[lo : lo + 256, :] = rows_dot(flat(x_all[:, :, lo : lo + 256]), flat(right[...])).astype(BF)

    for t in (1, 2, 3):
        for other in (1, 0):
            for way, peer, source in ((0, at.zp, at.zm), (1, at.zm, at.zp)):
                j = at.slab((4 - t) * (1 - 2 * way), other)
                total[...] = back(j)
                if t == 1:
                    sends.arrived(rhalf.at[way, other], rring_sem.at[0, way, other], source)
                    rows = pl.ds(64 * way, 64)
                    total[rows] = total[rows] + rhalf[way, other].astype(F32)
                else:
                    sends.arrived(rfull.at[t - 2, way, other], rring_sem.at[t - 1, way, other], source)
                    total[...] = total[...] + rfull[t - 2, way, other].astype(F32)
                rstage[t, way, other] = total[...].astype(BF)
                sends.go(
                    rstage.at[t, way, other],
                    rfull.at[t - 1, way, other],
                    rring_sem.at[t, way, other],
                    peer,
                )
        if t == 1:
            wgrad(gw, ga, 0)
        elif t == 2:
            wgrad(gw, ga, 256)
            down(512, 256)
        else:
            wgrad(uw, ub, 0)
    for other in (1, 0):
        j = at.slab(0, other)
        total[...] = back(j)
        for way, source in ((0, at.zm), (1, at.zp)):
            sends.arrived(rfull.at[2, way, other], rring_sem.at[3, way, other], source)
            total[...] = total[...] + rfull[2, way, other].astype(F32)
        if other == 1:
            rpair[0] = total[...].astype(BF)
            sends.go(rpair.at[0], rpair.at[1], rring_sem.at[4, 0, 0], at.hp)
    total[...] = total[...] + og[...].astype(F32)
    sends.arrived(rpair.at[1], rring_sem.at[4, 0, 0], at.hp)
    total[...] = total[...] + rpair[1].astype(F32)

    gr_out[...] = total[...].astype(BF)
    sends.go(gr_out.at[pl.ds(64, 64)], gr_rim.at[0], rim_sem.at[2], at.after)
    sends.go(gr_out.at[pl.ds(0, 64)], gr_rim.at[1], rim_sem.at[3], at.before)

    def tap_store(n, cut, value):
        tap_out[n // 2, n % 2 : n % 2 + 1, cut] = value

    tap_totals(total, frame, tap_store)
    tap_out[13, 1:2] = jnp.zeros((1, tap_out.shape[2]), F32)
    tap_out[14] = jnp.zeros(tap_out.shape[1:], F32)
    tap_out[15] = jnp.zeros(tap_out.shape[1:], F32)
    for n, peer in enumerate(row_peers):
        j = (at.r + n + 1) % 16
        sends.go(tap_out.at[j], tap_in.at[at.r], tap_sem.at[0, at.r], peer)
    for plane in (0, 1):
        fill_plane(
            gframe,
            plane + 1,
            lambda i: total[pl.ds(pl.multiple_of(plane * 64 + i * 16, 16), 16)],
        )
    wgrad(uw, ub, 256)
    down(768, 128)
    tap_in[at.r] = tap_out[at.r]
    for n, peer in enumerate(row_peers):
        j = (at.r + n + 1) % 16
        sends.arrived(tap_in.at[j], tap_sem.at[0, j], peer)
    tap_all[at.r] = jnp.sum(tap_in[...], axis=0)
    for n, peer in enumerate(row_peers):
        sends.go(tap_all.at[at.r], tap_all.at[at.r], tap_sem.at[1, at.r], peer)
    rims(gr_rim, rim_sem.at[pl.ds(2, 2)], gframe)

    def grads(i, value):
        pgrad[pl.ds(pl.multiple_of(i * 16, 16), 16)] = value.astype(BF)

    convolve(gframe, taps, True, lines, grads)
    for n, peer in enumerate(row_peers):
        j = (at.r + n + 1) % 16
        sends.arrived(tap_all.at[j], tap_sem.at[1, j], peer)
    for n in range(27):
        kgrad[n] = tap_all[n // 2, n % 2 : n % 2 + 1]
    sends.finish()


VM = pl.BlockSpec(memory_space=pltpu.VMEM)


def run(px, og, taps, gate, up, wg, wu, wd):
    feats, units = og.shape[1], gate.shape[1]
    tok, hid = (16, 128, feats), (16, 128, units)
    vm = pltpu.VMEM
    return pl.pallas_call(
        whole,
        out_shape=[
            jax.ShapeDtypeStruct((128, feats), BF),
            jax.ShapeDtypeStruct((27, 1, feats), F32),
            jax.ShapeDtypeStruct((feats, units), BF),
            jax.ShapeDtypeStruct((feats, units), BF),
            jax.ShapeDtypeStruct((units, feats), BF),
        ],
        in_specs=[VM] * 8,
        out_specs=[VM] * 5,
        scratch_shapes=[
            *(vm(s, BF) for s in (tok, tok, hid, hid, hid, hid, hid, hid)),
            vm((feats, units), BF),
            vm((units, feats), BF),
            vm((units, feats), BF),
            vm(hid, BF),
            vm((8, 128, units), BF),
            vm((4, 2, 128, units), BF),
            vm((2, 64, units), BF),
            vm((2, 64, units), BF),
            vm((2, 128, units), BF),
            vm((2, 128, units), BF),
            vm((128, units), BF),
            vm((4, 2, 2, 128, feats), BF),
            vm((2, 2, 64, feats), BF),
            vm((3, 2, 2, 128, feats), BF),
            vm((2, 128, feats), BF),
            vm((2, 64, feats), BF),
            vm((2, 64, feats), BF),
            vm((128, feats), BF),
            vm((3, 4, 10, 8, feats), F32),
            vm((3, 4, 10, 8, feats), F32),
            vm((16, feats), F32),
            vm((128, feats), F32),
            vm((16, 2, feats), F32),
            vm((16, 2, feats), F32),
            vm((16, 2, feats), F32),
            DMA((170,)),
            DMA((2, 16)),
            DMA((2, 16)),
            DMA((2, 16)),
            DMA((2, 16)),
            DMA((2, 16)),
            DMA((8,)),
            DMA((5, 2)),
            DMA((5, 2, 2)),
            DMA((4,)),
            DMA((2, 16)),
        ],
        compiler_params=pltpu.CompilerParams(
            collective_id=0, has_side_effects=True, vmem_limit_bytes=67043328
        ),
        name="whole",
    )(px, og, taps, gate, up, wg, wu, wd)


def body(patches, out_grad, conv_kernel, saved_gate, saved_up, w_gate, w_up, w_down):
    planes, height, breadth, features = patches.shape
    own = planes * height * breadth
    patch_grad, kernel_grad, gate_wgrad, up_wgrad, down_wgrad = run(
        patches.reshape(own, features),
        out_grad.reshape(own, features),
        conv_kernel.reshape(3, 3, 3, 1, features),
        saved_gate,
        saved_up,
        w_gate,
        w_up,
        w_down,
    )
    return (
        patch_grad.reshape(patches.shape),
        kernel_grad.reshape(conv_kernel.shape),
        gate_wgrad,
        up_wgrad,
        down_wgrad,
    )


def solution(mesh):
    return jax.shard_map(
        body,
        mesh=mesh,
        in_specs=(
            P("row", None, None, "col"),
            P("row", None, None, "col"),
            P(None, None, None, "col"),
            P("col", "row"),
            P("col", "row"),
            P("col", "row"),
            P("col", "row"),
            P("row", "col"),
        ),
        out_specs=(
            P("row", None, None, "col"),
            P(None, None, None, "col"),
            P("col", "row"),
            P("col", "row"),
            P("row", "col"),
        ),
        check_vma=False,
    )
```

```python
import jax
import jax.numpy as jnp
from jax import lax
from jax.experimental import pallas as pl
from jax.experimental.pallas import tpu as pltpu
from jax.sharding import PartitionSpec as P

MESH = pl.DeviceIdType.MESH
BF = jnp.bfloat16
F32 = jnp.float32
DMA = pltpu.SemaphoreType.DMA


class Sends:
    def __init__(self, sem):
        self.sem = sem

    def copy(self, src, dst, recv, device):
        return pltpu.make_async_remote_copy(
            src_ref=src,
            dst_ref=dst,
            send_sem=self.sem,
            recv_sem=recv,
            device_id=device,
            device_id_type=MESH,
        )

    def go(self, src, dst, recv, device):
        self.copy(src, dst, recv, device).start()

    def arrived(self, dst, recv, device):
        self.copy(dst, dst, recv, device).wait_recv()

    def finish(self, as_large, recv, device):
        self.copy(as_large, as_large, recv, device).wait_send()


class Place:
    def __init__(self):
        r, c = lax.axis_index("row"), lax.axis_index("col")
        self.r, self.c = r, c
        self.z, self.h = r // 2, r % 2
        self.x, self.l, self.k = c // 4, (c // 2) % 2, c % 2
        self.zp, self.zm = ((r + 2) % 16, c), ((r + 14) % 16, c)
        self.hp = (r + 1 - 2 * self.h, c)
        self.after, self.before = ((r + 1) % 16, c), ((r + 15) % 16, c)
        self.xp, self.xm = (r, (c + 4) % 16), (r, (c + 12) % 16)
        self.lp = (r, c + 2 - 4 * self.l)
        self.kp = (r, c + 1 - 2 * self.k)

    def slab(self, dz, other):
        hh = self.h + other * (1 - 2 * self.h)
        return ((self.z + dz + 8) % 8) * 2 + hh

    def tile(self, dx, other):
        return (self.x + dx + 4) % 4, self.l + other * (1 - 2 * self.l), self.k

    def number(self, t):
        return t[0] * 4 + t[1] * 2 + t[2]


class RowGather:
    def __init__(self, at, sends, buf, recv, base, n):
        self.at, self.sends, self.buf, self.recv, self.base, self.n = at, sends, buf, recv, base, n

    def ref(self, j, lo=0, size=None):
        return self.buf.at[j, pl.ds(self.base + lo, self.n if size is None else size)]

    def sem(self, way, s, other):
        return self.recv.at[8 * way + 2 * (s - 1) + other]

    def start(self, own):
        at, ref = self.at, self.ref(self.at.r)
        self.sends.go(own, ref, self.recv.at[16], at.hp)
        self.sends.go(own, ref, self.sem(0, 1, 0), at.zp)
        self.sends.go(own, ref, self.sem(1, 1, 0), at.zm)

    def wait(self, j, sem, lo=0, size=None):
        self.sends.arrived(self.ref(j, lo, size), sem, self.at.hp)

    def pair(self):
        at = self.at
        j = at.slab(0, 1)
        self.wait(j, self.recv.at[16])
        for peer, way in ((at.zp, 0), (at.zm, 1)):
            self.sends.go(self.ref(j), self.ref(j), self.sem(way, 1, 1), peer)
        return [j]

    def step(self, s):
        at, half, got = self.at, self.n // 2, []
        for other in (0, 1):
            if s == 4:
                j = at.slab(4, other)
                self.wait(j, self.sem(0, 4, other), 0, half)
                self.wait(j, self.sem(1, 4, other), half, half)
                got.append(j)
                continue
            for way, dz, peer in ((0, -s, at.zp), (1, s, at.zm)):
                j = at.slab(dz, other)
                self.wait(j, self.sem(way, s, other))
                ref = self.ref(j) if s < 3 else self.ref(j, half * way, half)
                self.sends.go(ref, ref, self.sem(way, s + 1, other), peer)
                got.append(j)
        return got

    def finish(self):
        sent = self.buf.at[pl.ds(0, 15), pl.ds(self.base, self.n)]
        self.sends.finish(sent, self.recv.at[16], self.at.hp)


class ColGather:
    def __init__(self, at, sends, buf, recv, base, n):
        self.at, self.sends, self.buf, self.recv, self.base, self.n = at, sends, buf, recv, base, n

    def ref(self, t, lo, size):
        return self.buf.at[self.at.number(t), pl.ds(self.base + lo, size)]

    def ring(self, way, s, other):
        return 4 * way + 2 * (s - 1) + other

    def move(self, t, sem, peer, lo=0, size=None, own=None):
        ref = self.ref(t, lo, self.n if size is None else size)
        self.sends.go(ref if own is None else own, ref, self.recv.at[sem], peer)

    def wait(self, t, sem, lo=0, size=None):
        ref = self.ref(t, lo, self.n if size is None else size)
        self.sends.arrived(ref, self.recv.at[sem], self.at.kp)

    def start(self, own=None):
        at, t = self.at, self.at.tile(0, 0)
        self.move(t, 12, at.lp, own=own)
        self.move(t, self.ring(0, 1, 0), at.xp, own=own)
        self.move(t, self.ring(1, 1, 0), at.xm, own=own)
        self.move(t, 11, at.kp, own=own)

    def pair(self):
        at, t, half = self.at, self.at.tile(0, 1), self.n // 2
        self.wait(t, 12)
        self.move(t, self.ring(0, 1, 1), at.xp, 0, half)
        self.move(t, self.ring(1, 1, 1), at.xm, 0, half)
        self.move(t, 11, at.kp)

    def step1(self):
        at, half, quarter = self.at, self.n // 2, self.n // 4
        for way, dx, peer in ((0, -1, at.xp), (1, 1, at.xm)):
            t = at.tile(dx, 0)
            self.wait(t, self.ring(way, 1, 0))
            self.move(t, self.ring(way, 2, 0), peer, half * way, half)
            self.move(t, 8 + way, at.lp, half, half)
            self.move(t, 11, at.kp)
        for way, dx, peer in ((0, -1, at.xp), (1, 1, at.xm)):
            t = at.tile(dx, 1)
            self.wait(t, self.ring(way, 1, 1), 0, half)
            self.move(t, self.ring(way, 2, 1), peer, quarter * way, quarter)

    def step2(self):
        at, half, quarter = self.at, self.n // 2, self.n // 4
        t = at.tile(2, 0)
        self.wait(t, self.ring(1, 2, 0), half, half)
        self.move(t, 10, at.lp, half, half)
        self.wait(t, self.ring(0, 2, 0), 0, half)
        self.move(t, 11, at.kp)
        for way, dx in ((0, -1), (1, 1)):
            t = at.tile(dx, 1)
            self.wait(t, 8 + way, half, half)
            self.move(t, 11, at.kp)
        t = at.tile(2, 1)
        self.wait(t, self.ring(0, 2, 1), 0, quarter)
        self.wait(t, self.ring(1, 2, 1), quarter, quarter)

    def step3(self):
        at, half = self.at, self.n // 2
        t = at.tile(2, 1)
        self.wait(t, 10, half, half)
        self.move(t, 11, at.kp)

    def many(self, tiles):
        return self.buf.at[pl.ds(0, tiles), pl.ds(self.base, self.n)]

    def rest(self):
        self.sends.arrived(self.many(8), self.recv.at[11], self.at.kp)

    def finish(self):
        self.sends.finish(self.many(15), self.recv.at[11], self.at.kp)


class ColReduce:
    def __init__(self, at, sends, mate_sends, base, part, mate, mate_sem, stage, halves, fulls, pair, sem, put):
        self.at, self.sends, self.mate_sends, self.base = at, sends, mate_sends, base
        self.part, self.mate, self.mate_sem = part, mate, mate_sem
        self.stage, self.halves, self.fulls, self.pair, self.sem, self.put = (
            stage, halves, fulls, pair, sem, put,
        )

    def ell(self, o):
        return self.at.l + o * (1 - 2 * self.at.l)

    def ex(self, dx):
        return (self.at.x + dx + 4) % 4

    def mated(self, dx, o):
        zz = self.ex(dx) * 2 + self.ell(o)
        self.mate_sends.arrived(
            self.mate.at[zz, pl.ds(self.base, 64)], self.mate_sem.at[zz], self.at.kp
        )
        return zz

    def summed(self, zz, lo, n):
        rows = pl.ds(self.base + lo, n)
        return self.part[2 * zz + self.at.k, rows].astype(F32) + self.mate[zz, rows].astype(F32)

    def stage1(self):
        at = self.at
        for o in (1, 0):
            ll = self.ell(o)
            j = self.mated(2, o)
            for lo in (0, 32):
                self.stage[0, o, lo : lo + 32] = self.summed(j, lo, 32).astype(BF)
            for way, peer in ((0, at.xp), (1, at.xm)):
                self.sends.go(
                    self.stage.at[0, o, pl.ds(32 * way, 32)],
                    self.halves.at[way, ll],
                    self.sem.at[way, ll],
                    peer,
                )

    def stage2(self):
        at = self.at
        for o in (1, 0):
            ll = self.ell(o)
            for way, peer, source in ((0, at.xp, at.xm), (1, at.xm, at.xp)):
                j = self.mated(1 - 2 * way, o)
                self.sends.arrived(self.halves.at[way, ll], self.sem.at[way, ll], source)
                lo = 32 * way
                self.stage[1 + way, o, lo : lo + 32] = (
                    self.summed(j, lo, 32) + self.halves[way, ll].astype(F32)
                ).astype(BF)
                lo = 32 - lo
                self.stage[1 + way, o, lo : lo + 32] = self.summed(j, lo, 32).astype(BF)
                self.sends.go(
                    self.stage.at[1 + way, o], self.fulls.at[way, ll], self.sem.at[2 + way, ll], peer
                )

    def full(self, o):
        at, ll = self.at, self.ell(o)
        j = self.mated(0, o)
        self.sends.arrived(self.fulls.at[0, ll], self.sem.at[2, ll], at.xm)
        self.sends.arrived(self.fulls.at[1, ll], self.sem.at[3, ll], at.xp)

        def value(lo):
            total = self.summed(j, lo, 32) + self.fulls[0, ll, lo : lo + 32].astype(F32)
            return total + self.fulls[1, ll, lo : lo + 32].astype(F32)

        return value

    def stage3(self):
        at = self.at
        value = self.full(1)
        for lo in (0, 32):
            self.stage[3, 0, lo : lo + 32] = value(lo).astype(BF)
        self.sends.go(self.stage.at[3, 0], self.pair, self.sem.at[4, 0], at.lp)

    def finish(self):
        rows = pl.ds(self.base, 64)
        self.sends.finish(self.part.at[pl.ds(0, 7), rows], self.sem.at[4, 0], self.at.lp)
        self.mate_sends.finish(self.mate.at[:, rows], self.mate_sem.at[0], self.at.kp)

    def stage4(self):
        value = self.full(0)
        self.sends.arrived(self.pair, self.sem.at[4, 0], self.at.lp)
        for lo in (0, 32):
            self.put(lo, (value(lo) + self.pair[lo : lo + 32].astype(F32)).astype(BF))


def shifts(line):
    at = lax.broadcasted_iota(jnp.int32, line.shape, 0)
    zero = jnp.zeros_like(line)
    return (
        jnp.where(at == 0, zero, pltpu.roll(line, 1, 0)),
        line,
        jnp.where(at == 7, zero, pltpu.roll(line, 7, 0)),
    )


def clear_rim(frame):
    zero = jnp.zeros(frame.shape[3:], F32)
    for e in range(3):
        for plane in range(4):
            frame[e, plane, 0] = zero
            frame[e, plane, 9] = zero


def fill_plane(frame, plane, read):
    def two(i, carry):
        rows = read(i)
        for half in range(2):
            for e, line in enumerate(shifts(rows[8 * half : 8 * half + 8])):
                frame[e, plane, 2 * i + half + 1] = line
        return carry

    lax.fori_loop(0, 4, two, 0)


def convolve(frame, taps, flipped, base, write):
    def line(i, carry):
        for half in range(2):
            y = 2 * i + half
            plane, y = y // 8, y % 8
            total = frame[1, plane + 1, y + 1]
            for a in range(3):
                for b in range(3):
                    for e in range(3):
                        ta, tb, te = (2 - a, 2 - b, 2 - e) if flipped else (a, b, e)
                        tap = taps[ta, tb, te : te + 1, :]
                        total = total + tap * frame[e, plane + a, y + b]
            base[8 * half : 8 * half + 8] = total
        write(i, base[...])
        return carry

    lax.fori_loop(0, 8, line, 0)


def tap_totals(grads, frame, plane, store):
    for lanes in range(0, grads.shape[1], 128):
        cut = pl.ds(lanes, 128)

        def line(i, totals):
            grad = grads[pl.ds(pl.multiple_of(plane * 64 + i * 8, 8), 8), cut]
            return tuple(
                totals[9 * a + 3 * b + e] + grad * frame[e, plane + a, i + b, :, cut]
                for a in range(3)
                for b in range(3)
                for e in range(3)
            )

        totals = lax.fori_loop(0, 8, line, tuple(jnp.zeros((8, 128), F32) for _ in range(27)))
        for n, total in enumerate(totals):
            store(n, cut, jnp.sum(total, axis=0, keepdims=True))


def rowwise(n, work):
    def some(i, carry):
        work(pl.ds(pl.multiple_of(i * 32, 32), 32))
        return carry

    lax.fori_loop(0, n // 32, some, 0)


def flat(value):
    return value.reshape(value.shape[0] * value.shape[1], value.shape[2])


def rows_dot(a, b):
    return lax.dot_general(a, b, (((0,), (0,)), ((), ())), preferred_element_type=F32)


def whole(
    px, og, taps, gate, up, wg, wu, wd,
    pgrad, kgrad, gw, uw, dw,
    dy_all, x_all, g_all, u_all, dh_all, hid, ga, ub,
    wdt, wgt, wut, part, mate, stage, halves, fulls, pairs,
    rstage, rhalf, rfull, rpair,
    px_rim, gr_rim, gr_out, frame, gframe, lines, total, tap_out, tap_in, tap_all,
    send_sem, dy_sem, x_sem, g_sem, u_sem, h_sem, mate_sem, ring_sem, rring_sem, rim_sem, tap_sem,
):
    at = Place()
    count = iter(range(send_sem.shape[0]))

    def stream():
        return Sends(send_sem.at[next(count)])

    rim_sends, first_taps, last_taps = stream(), stream(), stream()
    mate_sends, back_sends = [stream(), stream()], [stream(), stream()]
    barrier = pltpu.get_barrier_semaphore()
    row_peers = [((at.r + d) % 16, at.c) for d in range(1, 16)]
    peers = row_peers + [at.xp, at.xm, at.lp, at.kp]
    for peer in peers:
        pl.semaphore_signal(barrier, inc=1, device_id=peer, device_id_type=MESH)
    wdt[...] = wd[...].T
    dy_all[at.r] = og[...]
    g_all[at.c] = gate[...]
    u_all[at.c] = up[...]
    pl.semaphore_wait(barrier, len(peers))

    def reduce(q):
        def put(lo, value):
            dh_all[at.c, 64 * q + lo : 64 * q + lo + 32] = value

        return ColReduce(
            at, stream(), mate_sends[q], 64 * q, part, mate, mate_sem.at[q],
            stage.at[q], halves.at[q], fulls.at[q], pairs.at[q], ring_sem.at[q], put,
        )

    both = (0, 1)
    dy = [RowGather(at, stream(), dy_all, dy_sem.at[q], 64 * q, 64) for q in both]
    xg = RowGather(at, stream(), x_all, x_sem, 0, 128)
    gg = [ColGather(at, stream(), g_all, g_sem.at[q], 64 * q, 64) for q in both]
    ug = [ColGather(at, stream(), u_all, u_sem.at[q], 64 * q, 64) for q in both]
    hg = [ColGather(at, stream(), dh_all, h_sem.at[q], 64 * q, 64) for q in both]
    red = [reduce(q) for q in both]

    def chunk(ref, q):
        return ref.at[pl.ds(64 * q, 64)]

    def partials(q, slabs):
        rows = pl.ds(64 * q, 64)
        for j in slabs:
            part[j, rows] = jnp.dot(
                dy_all[j, rows], wdt[...], preferred_element_type=F32
            ).astype(BF)

    def to_mate(q, dz):
        zz = (at.z + dz + 8) % 8
        rows = pl.ds(64 * q, 64)
        mate_sends[q].go(
            part.at[2 * zz + 1 - at.k, rows], mate.at[zz, rows], mate_sem.at[q, zz], at.kp
        )

    def dy_step(q, s):
        partials(q, dy[q].step(s))
        to_mate(q, s)
        if s < 4:
            to_mate(q, -s)

    def rims(rim, sem, inside):
        for side, (peer, end) in enumerate(((at.before, 0), (at.after, 15))):
            rim_sends.arrived(rim.at[side], sem.at[side], peer)
            fill_plane(
                inside,
                3 * side,
                lambda i: jnp.where(
                    at.r == end, 0.0, rim[side, pl.ds(pl.multiple_of(i * 16, 16), 16)].astype(F32)
                ),
            )

    def swiglu(q):
        def work(i, carry):
            j, rows = i // 2, pl.ds(pl.multiple_of(64 * q + i % 2 * 32, 32), 32)
            g, u = g_all[j, rows].astype(F32), u_all[j, rows].astype(F32)
            s = 1.0 / (1.0 + jnp.exp(-g))
            silu = g * s
            hid[j, rows] = (silu * u).astype(BF)
            ga[j, rows] = (u * (s + silu * (1.0 - s))).astype(BF)
            ub[j, rows] = silu.astype(BF)
            return carry

        lax.fori_loop(0, 32, work, 0)

    def hidden_grads(q, first, n):
        def work(i, carry):
            j = (at.z * 2 + first + i // 2) % 16
            rows = pl.ds(pl.multiple_of(64 * q + i % 2 * 32, 32), 32)
            grad = dh_all[j, rows].astype(F32)
            ga[j, rows] = (ga[j, rows].astype(F32) * grad).astype(BF)
            ub[j, rows] = (ub[j, rows].astype(F32) * grad).astype(BF)
            return carry

        lax.fori_loop(0, 2 * n, work, 0)

    def down(lo, n):
        dw[lo : lo + n, :] = rows_dot(flat(hid[:, :, lo : lo + n]), flat(dy_all[...])).astype(BF)

    def wgrad(out, right, lo):
        out[lo : lo + 256, :] = rows_dot(flat(x_all[:, :, lo : lo + 256]), flat(right[...])).astype(BF)

    def back(q, j):
        rows = pl.ds(64 * q, 64)
        return jnp.dot(ga[j, rows], wgt[...], preferred_element_type=F32) + jnp.dot(
            ub[j, rows], wut[...], preferred_element_type=F32
        )

    ways = ((0, at.zp, at.zm), (1, at.zm, at.zp))

    def back_first(q):
        for other in (1, 0):
            value = back(q, at.slab(4, other))
            for way, peer, _ in ways:
                rows = pl.ds(32 * way, 32)
                rstage[q, 0, way, other, rows] = value[32 * way : 32 * way + 32].astype(BF)
                back_sends[q].go(
                    rstage.at[q, 0, way, other, rows],
                    rhalf.at[q, way, other],
                    rring_sem.at[q, 0, way, other],
                    peer,
                )

    def back_step(q, t):
        for other in (1, 0):
            for way, peer, source in ways:
                value = back(q, at.slab((4 - t) * (1 - 2 * way), other))
                out = rstage.at[q, t, way, other]
                if t == 1:
                    back_sends[q].arrived(rhalf.at[q, way, other], rring_sem.at[q, 0, way, other], source)
                    lo = 32 * way
                    out[lo : lo + 32] = (
                        value[lo : lo + 32] + rhalf[q, way, other].astype(F32)
                    ).astype(BF)
                    lo = 32 - lo
                    out[lo : lo + 32] = value[lo : lo + 32].astype(BF)
                else:
                    came = rfull.at[q, t - 2, way, other]
                    back_sends[q].arrived(came, rring_sem.at[q, t - 1, way, other], source)
                    out[...] = (value + came[...].astype(F32)).astype(BF)
                back_sends[q].go(
                    out, rfull.at[q, t - 1, way, other], rring_sem.at[q, t, way, other], peer
                )

    def back_last(q):
        rows = pl.ds(64 * q, 64)
        for other in (1, 0):
            value = back(q, at.slab(0, other))
            for way, _, source in ways:
                came = rfull.at[q, 2, way, other]
                back_sends[q].arrived(came, rring_sem.at[q, 3, way, other], source)
                value = value + came[...].astype(F32)
            if other == 1:
                rpair[q, 0] = value.astype(BF)
                back_sends[q].go(rpair.at[q, 0], rpair.at[q, 1], rring_sem.at[q, 4, 0, 0], at.hp)
            else:
                total[rows] = value + og[rows].astype(F32)

    def back_pair(q):
        rows = pl.ds(64 * q, 64)
        back_sends[q].arrived(rpair.at[q, 1], rring_sem.at[q, 4, 0, 0], at.hp)
        total[rows] = total[rows] + rpair[q, 1].astype(F32)
        gr_out[rows] = total[rows].astype(BF)
        rim_sends.go(
            chunk(gr_out, q), gr_rim.at[1 - q], rim_sem.at[3 - q], at.after if q else at.before
        )

    def fill():
        clear_rim(frame)
        for plane in (0, 1):
            fill_plane(
                frame,
                plane + 1,
                lambda i: px[pl.ds(pl.multiple_of(plane * 64 + i * 16, 16), 16)].astype(F32),
            )

    def mixed(i, value):
        x_all[at.r, pl.ds(pl.multiple_of(i * 16, 16), 16)] = value.astype(BF)

    def tap_store(plane, n, cut, value):
        spot = tap_out.at[n // 2, n % 2 : n % 2 + 1, cut]
        spot[...] = value if plane == 0 else spot[...] + value

    def taps_of(plane):
        tap_totals(total, frame, plane, lambda n, cut, value: tap_store(plane, n, cut, value))
        fill_plane(
            gframe,
            plane + 1,
            lambda i: total[pl.ds(pl.multiple_of(plane * 64 + i * 16, 16), 16)],
        )

    tap_out[13, 1:2] = jnp.zeros((1, tap_out.shape[2]), F32)
    tap_out[14] = jnp.zeros(tap_out.shape[1:], F32)
    tap_out[15] = jnp.zeros(tap_out.shape[1:], F32)
    dy[0].start(chunk(og, 0))
    dy[1].start(chunk(og, 1))
    rim_sends.go(px.at[pl.ds(64, 64)], px_rim.at[0], rim_sem.at[0], at.after)
    rim_sends.go(px.at[pl.ds(0, 64)], px_rim.at[1], rim_sem.at[1], at.before)

    gg[0].start(chunk(gate, 0))
    gg[1].start(chunk(gate, 1))
    ug[1].start(chunk(up, 1))
    ug[0].start(chunk(up, 0))
    fill()
    wgt[...] = wg[...].T
    wut[...] = wu[...].T
    partials(0, [at.r])
    partials(0, dy[0].pair())
    to_mate(0, 0)
    dy_step(0, 1)
    gg[0].pair()
    partials(1, [at.r])
    partials(1, dy[1].pair())
    to_mate(1, 0)
    rims(px_rim, rim_sem, frame)
    convolve(frame, taps, False, lines, mixed)
    gg[1].pair()
    dy_step(0, 2)
    dy_step(1, 1)
    ug[1].pair()
    gg[0].step1()
    gg[1].step1()
    dy_step(0, 3)
    ug[0].pair()
    ug[1].step1()
    gg[0].step2()
    dy_step(1, 2)
    dy_step(0, 4)
    red[0].stage1()
    ug[0].step1()
    dy_step(1, 3)
    ug[1].step2()
    red[0].stage2()
    xg.start(x_all.at[at.r])
    ug[1].step3()
    dy_step(1, 4)
    ug[0].step2()
    gg[1].step2()
    red[1].stage1()
    gg[0].step3()
    red[0].stage3()
    ug[1].rest()
    xg.pair()
    red[1].stage2()
    xg.step(1)
    red[0].stage4()
    hg[0].start()
    red[1].stage3()
    gg[1].step3()
    ug[0].step3()
    ug[0].rest()
    hg[0].pair()
    gg[1].rest()
    swiglu(1)
    red[1].stage4()
    hg[1].start()
    xg.step(2)
    gg[0].rest()
    swiglu(0)
    hg[0].step1()
    hg[1].pair()
    hg[0].step2()
    hg[1].step1()
    xg.step(3)
    hg[0].step3()
    hg[0].rest()
    hidden_grads(0, 8, 2)
    back_first(0)
    hg[1].step2()
    hidden_grads(0, 10, 14)
    back_step(0, 1)
    hg[1].step3()
    hg[1].rest()
    hidden_grads(1, 8, 2)
    back_first(1)
    xg.step(4)
    back_step(0, 2)
    hidden_grads(1, 10, 14)
    back_step(1, 1)
    down(0, 256)
    back_step(0, 3)
    back_step(1, 2)
    wgrad(gw, ga, 0)
    back_last(0)
    back_step(1, 3)
    wgrad(gw, ga, 256)
    back_pair(0)
    back_last(1)
    clear_rim(gframe)
    down(256, 256)
    taps_of(0)
    back_pair(1)
    taps_of(1)
    for n, peer in enumerate(row_peers):
        j = (at.r + n + 1) % 16
        first_taps.go(tap_out.at[j], tap_in.at[at.r], tap_sem.at[0], peer)
    wgrad(uw, ub, 0)
    tap_in[at.r] = tap_out[at.r]
    first_taps.arrived(tap_in.at[pl.ds(0, 15)], tap_sem.at[0], at.hp)
    tap_all[at.r] = jnp.sum(tap_in[...], axis=0)
    for peer in row_peers:
        last_taps.go(tap_all.at[at.r], tap_all.at[at.r], tap_sem.at[1], peer)
    rims(gr_rim, rim_sem.at[pl.ds(2, 2)], gframe)

    def grads(i, value):
        pgrad[pl.ds(pl.multiple_of(i * 16, 16), 16)] = value.astype(BF)

    convolve(gframe, taps, True, lines, grads)
    wgrad(uw, ub, 256)
    down(512, 256)
    down(768, 128)
    last_taps.arrived(tap_all.at[pl.ds(0, 15)], tap_sem.at[1], at.hp)
    for n in range(27):
        e = n % 3
        kgrad[n // 9, n // 3 % 3, e : e + 1, :] = tap_all[n // 2, n % 2 : n % 2 + 1]
    for gather in (*dy, xg, *gg, *ug, *hg, *red):
        gather.finish()
    for q in both:
        sent = x_all.at[pl.ds(0, 15), pl.ds(64 * q, 64)]
        back_sends[q].finish(sent, rring_sem.at[q, 4, 0, 0], at.hp)
    rim_sends.finish(x_all.at[pl.ds(0, 4), pl.ds(0, 64)], rim_sem.at[0], at.hp)
    first_taps.finish(tap_in.at[pl.ds(0, 15)], tap_sem.at[0], at.hp)
    last_taps.finish(tap_in.at[pl.ds(0, 15)], tap_sem.at[1], at.hp)


VM = pl.BlockSpec(memory_space=pltpu.VMEM)


def run(px, og, taps, gate, up, wg, wu, wd):
    feats, units = og.shape[1], gate.shape[1]
    tok, hid = (16, 128, feats), (16, 128, units)
    vm = pltpu.VMEM
    return pl.pallas_call(
        whole,
        out_shape=[
            jax.ShapeDtypeStruct((128, feats), BF),
            jax.ShapeDtypeStruct((3, 3, 3, feats), F32),
            jax.ShapeDtypeStruct((feats, units), BF),
            jax.ShapeDtypeStruct((feats, units), BF),
            jax.ShapeDtypeStruct((units, feats), BF),
        ],
        in_specs=[VM] * 8,
        out_specs=[VM] * 5,
        scratch_shapes=[
            *(vm(s, BF) for s in (tok, tok, hid, hid, hid, hid, hid, hid)),
            vm((feats, units), BF),
            vm((units, feats), BF),
            vm((units, feats), BF),
            vm(hid, BF),
            vm((8, 128, units), BF),
            vm((2, 4, 2, 64, units), BF),
            vm((2, 2, 2, 32, units), BF),
            vm((2, 2, 2, 64, units), BF),
            vm((2, 64, units), BF),
            vm((2, 4, 2, 2, 64, feats), BF),
            vm((2, 2, 2, 32, feats), BF),
            vm((2, 3, 2, 2, 64, feats), BF),
            vm((2, 2, 64, feats), BF),
            vm((2, 64, feats), BF),
            vm((2, 64, feats), BF),
            vm((128, feats), BF),
            vm((3, 4, 10, 8, feats), F32),
            vm((3, 4, 10, 8, feats), F32),
            vm((16, feats), F32),
            vm((128, feats), F32),
            vm((16, 2, feats), F32),
            vm((16, 2, feats), F32),
            vm((16, 2, feats), F32),
            DMA((18,)),
            DMA((2, 17)),
            DMA((17,)),
            DMA((2, 13)),
            DMA((2, 13)),
            DMA((2, 13)),
            DMA((2, 8)),
            DMA((2, 5, 2)),
            DMA((2, 5, 2, 2)),
            DMA((4,)),
            DMA((2,)),
        ],
        compiler_params=pltpu.CompilerParams(
            collective_id=0, has_side_effects=True, vmem_limit_bytes=67043328
        ),
        name="whole",
    )(px, og, taps, gate, up, wg, wu, wd)


def settle(*refs):
    ins, outs, held, (come, go) = refs[:5], refs[5:10], refs[10:15], refs[15:]
    into = [pltpu.make_async_copy(a, v, come.at[i]) for i, (a, v) in enumerate(zip(ins, held))]
    out = [pltpu.make_async_copy(v, b, go.at[i]) for i, (v, b) in enumerate(zip(held, outs))]
    for copy in into:
        copy.start()
    for first, second in zip(into, out):
        first.wait()
        second.start()
    for copy in out:
        copy.wait()


def run_settle(results):
    like = [(a.shape, a.dtype) for a in results]
    return pl.pallas_call(
        settle,
        out_shape=[jax.ShapeDtypeStruct(*a) for a in like],
        in_specs=[pl.BlockSpec(memory_space=pl.ANY)] * 5,
        out_specs=[pl.BlockSpec(memory_space=pl.ANY)] * 5,
        scratch_shapes=[*(pltpu.VMEM(*a) for a in like), DMA((5,)), DMA((5,))],
        name="settle",
    )(*results)


def body(patches, out_grad, conv_kernel, saved_gate, saved_up, w_gate, w_up, w_down):
    planes, height, breadth, features = patches.shape
    own = planes * height * breadth
    results = run(
        patches.reshape(own, features),
        out_grad.reshape(own, features),
        conv_kernel,
        saved_gate,
        saved_up,
        w_gate,
        w_up,
        w_down,
    )
    patch_grad, kernel_grad, gate_wgrad, up_wgrad, down_wgrad = run_settle(results)
    return (
        patch_grad.reshape(patches.shape),
        kernel_grad,
        gate_wgrad,
        up_wgrad,
        down_wgrad,
    )


def solution(mesh):
    return jax.shard_map(
        body,
        mesh=mesh,
        in_specs=(
            P("row", None, None, "col"),
            P("row", None, None, "col"),
            P(None, None, None, "col"),
            P("col", "row"),
            P("col", "row"),
            P("col", "row"),
            P("col", "row"),
            P("row", "col"),
        ),
        out_specs=(
            P("row", None, None, "col"),
            P(None, None, None, "col"),
            P("col", "row"),
            P("col", "row"),
            P("row", "col"),
        ),
        check_vma=False,
    )
```

```python
import jax
import jax.numpy as jnp
from jax import lax
from jax.experimental import pallas as pl
from jax.experimental.pallas import tpu as pltpu
from jax.sharding import PartitionSpec as P

MESH = pl.DeviceIdType.MESH
BF = jnp.bfloat16
F32 = jnp.float32
DMA = pltpu.SemaphoreType.DMA


class Sends:
    def __init__(self, sem):
        self.sem = sem

    def copy(self, src, dst, recv, device):
        return pltpu.make_async_remote_copy(
            src_ref=src,
            dst_ref=dst,
            send_sem=self.sem,
            recv_sem=recv,
            device_id=device,
            device_id_type=MESH,
        )

    def go(self, src, dst, recv, device):
        self.copy(src, dst, recv, device).start()

    def arrived(self, dst, recv, device):
        self.copy(dst, dst, recv, device).wait_recv()

    def finish(self, as_large, recv, device):
        self.copy(as_large, as_large, recv, device).wait_send()


class Place:
    def __init__(self):
        r, c = lax.axis_index("row"), lax.axis_index("col")
        self.r, self.c = r, c
        self.z, self.h = r // 2, r % 2
        self.x, self.l, self.k = c // 4, (c // 2) % 2, c % 2
        self.zp, self.zm = ((r + 2) % 16, c), ((r + 14) % 16, c)
        self.hp = (r + 1 - 2 * self.h, c)
        self.after, self.before = ((r + 1) % 16, c), ((r + 15) % 16, c)
        self.xp, self.xm = (r, (c + 4) % 16), (r, (c + 12) % 16)
        self.lp = (r, c + 2 - 4 * self.l)
        self.kp = (r, c + 1 - 2 * self.k)

    def slab(self, dz, other):
        hh = self.h + other * (1 - 2 * self.h)
        return ((self.z + dz + 8) % 8) * 2 + hh

    def tile(self, dx, other):
        return (self.x + dx + 4) % 4, self.l + other * (1 - 2 * self.l), self.k

    def number(self, t):
        return t[0] * 4 + t[1] * 2 + t[2]


class RowGather:
    def __init__(self, at, sends, buf, recv, base, n):
        self.at, self.sends, self.buf, self.recv, self.base, self.n = at, sends, buf, recv, base, n

    def ref(self, j, lo=0, size=None):
        return self.buf.at[j, pl.ds(self.base + lo, self.n if size is None else size)]

    def sem(self, way, s, other):
        return self.recv.at[8 * way + 2 * (s - 1) + other]

    def start(self, own):
        at, ref = self.at, self.ref(self.at.r)
        self.sends.go(own, ref, self.recv.at[16], at.hp)
        self.sends.go(own, ref, self.sem(0, 1, 0), at.zp)
        self.sends.go(own, ref, self.sem(1, 1, 0), at.zm)

    def wait(self, j, sem, lo=0, size=None):
        self.sends.arrived(self.ref(j, lo, size), sem, self.at.hp)

    def pair(self):
        at = self.at
        j = at.slab(0, 1)
        self.wait(j, self.recv.at[16])
        for peer, way in ((at.zp, 0), (at.zm, 1)):
            self.sends.go(self.ref(j), self.ref(j), self.sem(way, 1, 1), peer)
        return [j]

    def step(self, s):
        at, half, got = self.at, self.n // 2, []
        for other in (0, 1):
            if s == 4:
                j = at.slab(4, other)
                self.wait(j, self.sem(0, 4, other), 0, half)
                self.wait(j, self.sem(1, 4, other), half, half)
                got.append(j)
                continue
            for way, dz, peer in ((0, -s, at.zp), (1, s, at.zm)):
                j = at.slab(dz, other)
                self.wait(j, self.sem(way, s, other))
                ref = self.ref(j) if s < 3 else self.ref(j, half * way, half)
                self.sends.go(ref, ref, self.sem(way, s + 1, other), peer)
                got.append(j)
        return got

    def finish(self):
        sent = self.buf.at[pl.ds(0, 15), pl.ds(self.base, self.n)]
        self.sends.finish(sent, self.recv.at[16], self.at.hp)


class ColGather:
    def __init__(self, at, sends, buf, recv, base, n):
        self.at, self.sends, self.buf, self.recv, self.base, self.n = at, sends, buf, recv, base, n

    def ref(self, t, lo, size):
        return self.buf.at[self.at.number(t), pl.ds(self.base + lo, size)]

    def ring(self, way, s, other):
        return 4 * way + 2 * (s - 1) + other

    def move(self, t, sem, peer, lo=0, size=None, own=None):
        ref = self.ref(t, lo, self.n if size is None else size)
        self.sends.go(ref if own is None else own, ref, self.recv.at[sem], peer)

    def wait(self, t, sem, lo=0, size=None):
        ref = self.ref(t, lo, self.n if size is None else size)
        self.sends.arrived(ref, self.recv.at[sem], self.at.kp)

    def start(self, own=None):
        at, t = self.at, self.at.tile(0, 0)
        self.move(t, 12, at.lp, own=own)
        self.move(t, self.ring(0, 1, 0), at.xp, own=own)
        self.move(t, self.ring(1, 1, 0), at.xm, own=own)
        self.move(t, 11, at.kp, own=own)

    def pair(self):
        at, t, half = self.at, self.at.tile(0, 1), self.n // 2
        self.wait(t, 12)
        self.move(t, self.ring(0, 1, 1), at.xp, 0, half)
        self.move(t, self.ring(1, 1, 1), at.xm, 0, half)
        self.move(t, 11, at.kp)

    def step1(self):
        at, half, quarter = self.at, self.n // 2, self.n // 4
        for way, dx, peer in ((0, -1, at.xp), (1, 1, at.xm)):
            t = at.tile(dx, 0)
            self.wait(t, self.ring(way, 1, 0))
            self.move(t, self.ring(way, 2, 0), peer, half * way, half)
            self.move(t, 8 + way, at.lp, half, half)
            self.move(t, 11, at.kp)
        for way, dx, peer in ((0, -1, at.xp), (1, 1, at.xm)):
            t = at.tile(dx, 1)
            self.wait(t, self.ring(way, 1, 1), 0, half)
            self.move(t, self.ring(way, 2, 1), peer, quarter * way, quarter)

    def step2(self):
        at, half, quarter = self.at, self.n // 2, self.n // 4
        t = at.tile(2, 0)
        self.wait(t, self.ring(1, 2, 0), half, half)
        self.move(t, 10, at.lp, half, half)
        self.wait(t, self.ring(0, 2, 0), 0, half)
        self.move(t, 11, at.kp)
        for way, dx in ((0, -1), (1, 1)):
            t = at.tile(dx, 1)
            self.wait(t, 8 + way, half, half)
            self.move(t, 11, at.kp)
        t = at.tile(2, 1)
        self.wait(t, self.ring(0, 2, 1), 0, quarter)
        self.wait(t, self.ring(1, 2, 1), quarter, quarter)

    def step3(self):
        at, half = self.at, self.n // 2
        t = at.tile(2, 1)
        self.wait(t, 10, half, half)
        self.move(t, 11, at.kp)

    def many(self, tiles):
        return self.buf.at[pl.ds(0, tiles), pl.ds(self.base, self.n)]

    def rest(self):
        self.sends.arrived(self.many(8), self.recv.at[11], self.at.kp)

    def finish(self):
        self.sends.finish(self.many(15), self.recv.at[11], self.at.kp)


class ColReduce:
    def __init__(self, at, sends, mate_sends, base, part, mate, mate_sem, stage, halves, fulls, pair, sem, put):
        self.at, self.sends, self.mate_sends, self.base = at, sends, mate_sends, base
        self.part, self.mate, self.mate_sem = part, mate, mate_sem
        self.stage, self.halves, self.fulls, self.pair, self.sem, self.put = (
            stage, halves, fulls, pair, sem, put,
        )

    def ell(self, o):
        return self.at.l + o * (1 - 2 * self.at.l)

    def ex(self, dx):
        return (self.at.x + dx + 4) % 4

    def mated(self, dx, o):
        zz = self.ex(dx) * 2 + self.ell(o)
        self.mate_sends.arrived(
            self.mate.at[zz, pl.ds(self.base, 64)], self.mate_sem.at[zz], self.at.kp
        )
        return zz

    def summed(self, zz, lo, n):
        rows = pl.ds(self.base + lo, n)
        return self.part[2 * zz + self.at.k, rows].astype(F32) + self.mate[zz, rows].astype(F32)

    def stage1(self):
        at = self.at
        for o in (1, 0):
            ll = self.ell(o)
            j = self.mated(2, o)
            for lo in (0, 32):
                self.stage[0, o, lo : lo + 32] = self.summed(j, lo, 32).astype(BF)
            for way, peer in ((0, at.xp), (1, at.xm)):
                self.sends.go(
                    self.stage.at[0, o, pl.ds(32 * way, 32)],
                    self.halves.at[way, ll],
                    self.sem.at[way, ll],
                    peer,
                )

    def stage2(self):
        at = self.at
        for o in (1, 0):
            ll = self.ell(o)
            for way, peer, source in ((0, at.xp, at.xm), (1, at.xm, at.xp)):
                j = self.mated(1 - 2 * way, o)
                self.sends.arrived(self.halves.at[way, ll], self.sem.at[way, ll], source)
                lo = 32 * way
                self.stage[1 + way, o, lo : lo + 32] = (
                    self.summed(j, lo, 32) + self.halves[way, ll].astype(F32)
                ).astype(BF)
                lo = 32 - lo
                self.stage[1 + way, o, lo : lo + 32] = self.summed(j, lo, 32).astype(BF)
                self.sends.go(
                    self.stage.at[1 + way, o], self.fulls.at[way, ll], self.sem.at[2 + way, ll], peer
                )

    def full(self, o):
        at, ll = self.at, self.ell(o)
        j = self.mated(0, o)
        self.sends.arrived(self.fulls.at[0, ll], self.sem.at[2, ll], at.xm)
        self.sends.arrived(self.fulls.at[1, ll], self.sem.at[3, ll], at.xp)

        def value(lo):
            total = self.summed(j, lo, 32) + self.fulls[0, ll, lo : lo + 32].astype(F32)
            return total + self.fulls[1, ll, lo : lo + 32].astype(F32)

        return value

    def stage3(self):
        at = self.at
        value = self.full(1)
        for lo in (0, 32):
            self.stage[3, 0, lo : lo + 32] = value(lo).astype(BF)
        self.sends.go(self.stage.at[3, 0], self.pair, self.sem.at[4, 0], at.lp)

    def finish(self):
        rows = pl.ds(self.base, 64)
        self.sends.finish(self.part.at[pl.ds(0, 7), rows], self.sem.at[4, 0], self.at.lp)
        self.mate_sends.finish(self.mate.at[:, rows], self.mate_sem.at[0], self.at.kp)

    def stage4(self):
        value = self.full(0)
        self.sends.arrived(self.pair, self.sem.at[4, 0], self.at.lp)
        for lo in (0, 32):
            self.put(lo, (value(lo) + self.pair[lo : lo + 32].astype(F32)).astype(BF))


def shifts(line):
    at = lax.broadcasted_iota(jnp.int32, line.shape, 0)
    zero = jnp.zeros_like(line)
    return (
        jnp.where(at == 0, zero, pltpu.roll(line, 1, 0)),
        line,
        jnp.where(at == 7, zero, pltpu.roll(line, 7, 0)),
    )


def clear_rim(frame):
    zero = jnp.zeros(frame.shape[3:], F32)
    for e in range(3):
        for plane in range(4):
            frame[e, plane, 0] = zero
            frame[e, plane, 9] = zero


def fill_plane(frame, plane, read):
    def two(i, carry):
        rows = read(i)
        for half in range(2):
            for e, line in enumerate(shifts(rows[8 * half : 8 * half + 8])):
                frame[e, plane, 2 * i + half + 1] = line
        return carry

    lax.fori_loop(0, 4, two, 0)


def convolve(frame, taps, flipped, base, write):
    def line(i, carry):
        for half in range(2):
            y = 2 * i + half
            plane, y = y // 8, y % 8
            total = frame[1, plane + 1, y + 1]
            for a in range(3):
                for b in range(3):
                    for e in range(3):
                        ta, tb, te = (2 - a, 2 - b, 2 - e) if flipped else (a, b, e)
                        tap = taps[ta, tb, te : te + 1, :]
                        total = total + tap * frame[e, plane + a, y + b]
            base[8 * half : 8 * half + 8] = total
        write(i, base[...])
        return carry

    lax.fori_loop(0, 8, line, 0)


def tap_totals(grads, frame, plane, store):
    for lanes in range(0, grads.shape[1], 128):
        cut = pl.ds(lanes, 128)

        def line(i, totals):
            grad = grads[pl.ds(pl.multiple_of(plane * 64 + i * 8, 8), 8), cut]
            return tuple(
                totals[9 * a + 3 * b + e] + grad * frame[e, plane + a, i + b, :, cut]
                for a in range(3)
                for b in range(3)
                for e in range(3)
            )

        totals = lax.fori_loop(0, 8, line, tuple(jnp.zeros((8, 128), F32) for _ in range(27)))
        for n, total in enumerate(totals):
            store(n, cut, jnp.sum(total, axis=0, keepdims=True))


def rowwise(n, work):
    def some(i, carry):
        work(pl.ds(pl.multiple_of(i * 32, 32), 32))
        return carry

    lax.fori_loop(0, n // 32, some, 0)


def flat(value):
    return value.reshape(value.shape[0] * value.shape[1], value.shape[2])


def rows_dot(a, b):
    return lax.dot_general(a, b, (((0,), (0,)), ((), ())), preferred_element_type=F32)


def whole(
    px, og, taps, gate, up, wg, wu, wd,
    pgrad, kgrad, gw, uw, dw,
    dy_all, x_all, g_all, u_all, dh_all, hid, ga, ub,
    wdt, wgt, wut, part, mate, stage, halves, fulls, pairs,
    rstage, rhalf, rfull, rpair,
    px_rim, gr_rim, gr_out, frame, gframe, lines, total, tap_out, tap_in, tap_all,
    send_sem, dy_sem, x_sem, g_sem, u_sem, h_sem, mate_sem, ring_sem, rring_sem, rim_sem, tap_sem,
):
    at = Place()
    count = iter(range(send_sem.shape[0]))

    def stream():
        return Sends(send_sem.at[next(count)])

    rim_sends, first_taps, last_taps = stream(), stream(), stream()
    mate_sends, back_sends = [stream(), stream()], [stream(), stream()]
    barrier = pltpu.get_barrier_semaphore()
    row_peers = [((at.r + d) % 16, at.c) for d in range(1, 16)]
    peers = [at.zp, at.zm, at.before, at.after, at.xp, at.xm, at.lp, at.kp]
    for peer in peers:
        pl.semaphore_signal(barrier, inc=1, device_id=peer, device_id_type=MESH)
    wdt[...] = wd[...].T
    dy_all[at.r] = og[...]
    g_all[at.c] = gate[...]
    u_all[at.c] = up[...]

    def reduce(q):
        def put(lo, value):
            dh_all[at.c, 64 * q + lo : 64 * q + lo + 32] = value

        return ColReduce(
            at, stream(), mate_sends[q], 64 * q, part, mate, mate_sem.at[q],
            stage.at[q], halves.at[q], fulls.at[q], pairs.at[q], ring_sem.at[q], put,
        )

    both = (0, 1)
    dy = [RowGather(at, stream(), dy_all, dy_sem.at[q], 64 * q, 64) for q in both]
    xg = RowGather(at, stream(), x_all, x_sem, 0, 128)
    gg = [ColGather(at, stream(), g_all, g_sem.at[q], 64 * q, 64) for q in both]
    ug = [ColGather(at, stream(), u_all, u_sem.at[q], 64 * q, 64) for q in both]
    hg = [ColGather(at, stream(), dh_all, h_sem.at[q], 64 * q, 64) for q in both]
    red = [reduce(q) for q in both]

    def chunk(ref, q):
        return ref.at[pl.ds(64 * q, 64)]

    def partials(q, slabs):
        rows = pl.ds(64 * q, 64)
        for j in slabs:
            part[j, rows] = jnp.dot(
                dy_all[j, rows], wdt[...], preferred_element_type=F32
            ).astype(BF)

    def to_mate(q, dz):
        zz = (at.z + dz + 8) % 8
        rows = pl.ds(64 * q, 64)
        mate_sends[q].go(
            part.at[2 * zz + 1 - at.k, rows], mate.at[zz, rows], mate_sem.at[q, zz], at.kp
        )

    def dy_step(q, s):
        partials(q, dy[q].step(s))
        to_mate(q, s)
        if s < 4:
            to_mate(q, -s)

    def rims(rim, sem, inside):
        for side, (peer, end) in enumerate(((at.before, 0), (at.after, 15))):
            rim_sends.arrived(rim.at[side], sem.at[side], peer)
            fill_plane(
                inside,
                3 * side,
                lambda i: jnp.where(
                    at.r == end, 0.0, rim[side, pl.ds(pl.multiple_of(i * 16, 16), 16)].astype(F32)
                ),
            )

    def swiglu(q):
        def work(i, carry):
            j, rows = i // 2, pl.ds(pl.multiple_of(64 * q + i % 2 * 32, 32), 32)
            g, u = g_all[j, rows].astype(F32), u_all[j, rows].astype(F32)
            s = 1.0 / (1.0 + jnp.exp(-g))
            silu = g * s
            hid[j, rows] = (silu * u).astype(BF)
            ga[j, rows] = (u * (s + silu * (1.0 - s))).astype(BF)
            ub[j, rows] = silu.astype(BF)
            return carry

        lax.fori_loop(0, 32, work, 0)

    def hidden_grads(q, first, n):
        def work(i, carry):
            j = (at.z * 2 + first + i // 2) % 16
            rows = pl.ds(pl.multiple_of(64 * q + i % 2 * 32, 32), 32)
            grad = dh_all[j, rows].astype(F32)
            ga[j, rows] = (ga[j, rows].astype(F32) * grad).astype(BF)
            ub[j, rows] = (ub[j, rows].astype(F32) * grad).astype(BF)
            return carry

        lax.fori_loop(0, 2 * n, work, 0)

    def down(lo, n):
        dw[lo : lo + n, :] = rows_dot(flat(hid[:, :, lo : lo + n]), flat(dy_all[...])).astype(BF)

    def wgrad(out, right, lo):
        out[lo : lo + 256, :] = rows_dot(flat(x_all[:, :, lo : lo + 256]), flat(right[...])).astype(BF)

    def back(q, j):
        rows = pl.ds(64 * q, 64)
        return jnp.dot(ga[j, rows], wgt[...], preferred_element_type=F32) + jnp.dot(
            ub[j, rows], wut[...], preferred_element_type=F32
        )

    ways = ((0, at.zp, at.zm), (1, at.zm, at.zp))

    def back_first(q):
        for other in (1, 0):
            value = back(q, at.slab(4, other))
            for way, peer, _ in ways:
                rows = pl.ds(32 * way, 32)
                rstage[q, 0, way, other, rows] = value[32 * way : 32 * way + 32].astype(BF)
                back_sends[q].go(
                    rstage.at[q, 0, way, other, rows],
                    rhalf.at[q, way, other],
                    rring_sem.at[q, 0, way, other],
                    peer,
                )

    def back_step(q, t):
        for other in (1, 0):
            for way, peer, source in ways:
                value = back(q, at.slab((4 - t) * (1 - 2 * way), other))
                out = rstage.at[q, t, way, other]
                if t == 1:
                    back_sends[q].arrived(rhalf.at[q, way, other], rring_sem.at[q, 0, way, other], source)
                    lo = 32 * way
                    out[lo : lo + 32] = (
                        value[lo : lo + 32] + rhalf[q, way, other].astype(F32)
                    ).astype(BF)
                    lo = 32 - lo
                    out[lo : lo + 32] = value[lo : lo + 32].astype(BF)
                else:
                    came = rfull.at[q, t - 2, way, other]
                    back_sends[q].arrived(came, rring_sem.at[q, t - 1, way, other], source)
                    out[...] = (value + came[...].astype(F32)).astype(BF)
                back_sends[q].go(
                    out, rfull.at[q, t - 1, way, other], rring_sem.at[q, t, way, other], peer
                )

    def back_last(q):
        rows = pl.ds(64 * q, 64)
        for other in (1, 0):
            value = back(q, at.slab(0, other))
            for way, _, source in ways:
                came = rfull.at[q, 2, way, other]
                back_sends[q].arrived(came, rring_sem.at[q, 3, way, other], source)
                value = value + came[...].astype(F32)
            if other == 1:
                rpair[q, 0] = value.astype(BF)
                back_sends[q].go(rpair.at[q, 0], rpair.at[q, 1], rring_sem.at[q, 4, 0, 0], at.hp)
            else:
                total[rows] = value + og[rows].astype(F32)

    def back_pair(q):
        rows = pl.ds(64 * q, 64)
        back_sends[q].arrived(rpair.at[q, 1], rring_sem.at[q, 4, 0, 0], at.hp)
        total[rows] = total[rows] + rpair[q, 1].astype(F32)
        gr_out[rows] = total[rows].astype(BF)
        rim_sends.go(
            chunk(gr_out, q), gr_rim.at[1 - q], rim_sem.at[3 - q], at.after if q else at.before
        )

    def fill():
        clear_rim(frame)
        for plane in (0, 1):
            fill_plane(
                frame,
                plane + 1,
                lambda i: px[pl.ds(pl.multiple_of(plane * 64 + i * 16, 16), 16)].astype(F32),
            )

    def mixed(i, value):
        x_all[at.r, pl.ds(pl.multiple_of(i * 16, 16), 16)] = value.astype(BF)

    def tap_store(plane, n, cut, value):
        spot = tap_out.at[n // 2, n % 2 : n % 2 + 1, cut]
        spot[...] = value if plane == 0 else spot[...] + value

    def taps_of(plane):
        tap_totals(total, frame, plane, lambda n, cut, value: tap_store(plane, n, cut, value))
        fill_plane(
            gframe,
            plane + 1,
            lambda i: total[pl.ds(pl.multiple_of(plane * 64 + i * 16, 16), 16)],
        )

    tap_out[13, 1:2] = jnp.zeros((1, tap_out.shape[2]), F32)
    tap_out[14] = jnp.zeros(tap_out.shape[1:], F32)
    tap_out[15] = jnp.zeros(tap_out.shape[1:], F32)
    wgt[...] = wg[...].T
    wut[...] = wu[...].T
    fill()
    clear_rim(gframe)
    partials(0, [at.r])
    partials(1, [at.r])
    pl.semaphore_wait(barrier, len(peers))
    dy[0].start(chunk(og, 0))
    dy[1].start(chunk(og, 1))
    rim_sends.go(px.at[pl.ds(64, 64)], px_rim.at[0], rim_sem.at[0], at.after)
    rim_sends.go(px.at[pl.ds(0, 64)], px_rim.at[1], rim_sem.at[1], at.before)

    gg[0].start(chunk(gate, 0))
    gg[1].start(chunk(gate, 1))
    ug[1].start(chunk(up, 1))
    ug[0].start(chunk(up, 0))
    partials(0, dy[0].pair())
    to_mate(0, 0)
    dy_step(0, 1)
    gg[0].pair()
    partials(1, dy[1].pair())
    to_mate(1, 0)
    rims(px_rim, rim_sem, frame)
    convolve(frame, taps, False, lines, mixed)
    gg[1].pair()
    dy_step(0, 2)
    dy_step(1, 1)
    ug[1].pair()
    gg[0].step1()
    gg[1].step1()
    dy_step(0, 3)
    ug[0].pair()
    ug[1].step1()
    gg[0].step2()
    dy_step(1, 2)
    dy_step(0, 4)
    red[0].stage1()
    ug[0].step1()
    dy_step(1, 3)
    ug[1].step2()
    red[0].stage2()
    xg.start(x_all.at[at.r])
    ug[1].step3()
    dy_step(1, 4)
    ug[0].step2()
    gg[1].step2()
    red[1].stage1()
    gg[0].step3()
    red[0].stage3()
    ug[1].rest()
    xg.pair()
    red[1].stage2()
    xg.step(1)
    red[0].stage4()
    hg[0].start()
    red[1].stage3()
    gg[1].step3()
    ug[0].step3()
    ug[0].rest()
    hg[0].pair()
    gg[1].rest()
    swiglu(1)
    red[1].stage4()
    hg[1].start()
    xg.step(2)
    gg[0].rest()
    swiglu(0)
    hg[0].step1()
    hg[1].pair()
    hg[0].step2()
    hg[1].step1()
    xg.step(3)
    hg[0].step3()
    hg[0].rest()
    hidden_grads(0, 8, 2)
    back_first(0)
    hg[1].step2()
    hidden_grads(0, 10, 14)
    back_step(0, 1)
    hg[1].step3()
    hg[1].rest()
    hidden_grads(1, 8, 2)
    back_first(1)
    xg.step(4)
    back_step(0, 2)
    hidden_grads(1, 10, 14)
    back_step(1, 1)
    down(0, 256)
    back_step(0, 3)
    back_step(1, 2)
    wgrad(gw, ga, 0)
    back_last(0)
    back_step(1, 3)
    wgrad(gw, ga, 256)
    back_pair(0)
    back_last(1)
    down(256, 256)
    taps_of(0)
    back_pair(1)
    taps_of(1)
    for n, peer in enumerate(row_peers):
        j = (at.r + n + 1) % 16
        first_taps.go(tap_out.at[j], tap_in.at[at.r], tap_sem.at[0], peer)
    wgrad(uw, ub, 0)
    tap_in[at.r] = tap_out[at.r]
    first_taps.arrived(tap_in.at[pl.ds(0, 15)], tap_sem.at[0], at.hp)
    tap_all[at.r] = jnp.sum(tap_in[...], axis=0)
    for peer in row_peers:
        last_taps.go(tap_all.at[at.r], tap_all.at[at.r], tap_sem.at[1], peer)
    rims(gr_rim, rim_sem.at[pl.ds(2, 2)], gframe)

    def grads(i, value):
        pgrad[pl.ds(pl.multiple_of(i * 16, 16), 16)] = value.astype(BF)

    convolve(gframe, taps, True, lines, grads)
    wgrad(uw, ub, 256)
    down(512, 256)
    down(768, 128)
    last_taps.arrived(tap_all.at[pl.ds(0, 15)], tap_sem.at[1], at.hp)
    for n in range(27):
        e = n % 3
        kgrad[n // 9, n // 3 % 3, e : e + 1, :] = tap_all[n // 2, n % 2 : n % 2 + 1]
    for gather in (*dy, xg, *gg, *ug, *hg, *red):
        gather.finish()
    for q in both:
        sent = x_all.at[pl.ds(0, 15), pl.ds(64 * q, 64)]
        back_sends[q].finish(sent, rring_sem.at[q, 4, 0, 0], at.hp)
    rim_sends.finish(x_all.at[pl.ds(0, 4), pl.ds(0, 64)], rim_sem.at[0], at.hp)
    first_taps.finish(tap_in.at[pl.ds(0, 15)], tap_sem.at[0], at.hp)
    last_taps.finish(tap_in.at[pl.ds(0, 15)], tap_sem.at[1], at.hp)


VM = pl.BlockSpec(memory_space=pltpu.VMEM)


def run(px, og, taps, gate, up, wg, wu, wd):
    feats, units = og.shape[1], gate.shape[1]
    tok, hid = (16, 128, feats), (16, 128, units)
    vm = pltpu.VMEM
    return pl.pallas_call(
        whole,
        out_shape=[
            jax.ShapeDtypeStruct((128, feats), BF),
            jax.ShapeDtypeStruct((3, 3, 3, feats), F32),
            jax.ShapeDtypeStruct((feats, units), BF),
            jax.ShapeDtypeStruct((feats, units), BF),
            jax.ShapeDtypeStruct((units, feats), BF),
        ],
        in_specs=[VM] * 8,
        out_specs=[VM] * 5,
        scratch_shapes=[
            *(vm(s, BF) for s in (tok, tok, hid, hid, hid, hid, hid, hid)),
            vm((feats, units), BF),
            vm((units, feats), BF),
            vm((units, feats), BF),
            vm(hid, BF),
            vm((8, 128, units), BF),
            vm((2, 4, 2, 64, units), BF),
            vm((2, 2, 2, 32, units), BF),
            vm((2, 2, 2, 64, units), BF),
            vm((2, 64, units), BF),
            vm((2, 4, 2, 2, 64, feats), BF),
            vm((2, 2, 2, 32, feats), BF),
            vm((2, 3, 2, 2, 64, feats), BF),
            vm((2, 2, 64, feats), BF),
            vm((2, 64, feats), BF),
            vm((2, 64, feats), BF),
            vm((128, feats), BF),
            vm((3, 4, 10, 8, feats), F32),
            vm((3, 4, 10, 8, feats), F32),
            vm((16, feats), F32),
            vm((128, feats), F32),
            vm((16, 2, feats), F32),
            vm((16, 2, feats), F32),
            vm((16, 2, feats), F32),
            DMA((18,)),
            DMA((2, 17)),
            DMA((17,)),
            DMA((2, 13)),
            DMA((2, 13)),
            DMA((2, 13)),
            DMA((2, 8)),
            DMA((2, 5, 2)),
            DMA((2, 5, 2, 2)),
            DMA((4,)),
            DMA((2,)),
        ],
        compiler_params=pltpu.CompilerParams(
            collective_id=0, has_side_effects=True, vmem_limit_bytes=67043328
        ),
        name="whole",
    )(px, og, taps, gate, up, wg, wu, wd)


def settle(*refs):
    ins, outs, held, (come, go) = refs[:5], refs[5:10], refs[10:15], refs[15:]
    into = [pltpu.make_async_copy(a, v, come.at[i]) for i, (a, v) in enumerate(zip(ins, held))]
    out = [pltpu.make_async_copy(v, b, go.at[i]) for i, (v, b) in enumerate(zip(held, outs))]
    for copy in into:
        copy.start()
    for first, second in zip(into, out):
        first.wait()
        second.start()
    for copy in out:
        copy.wait()


def run_settle(results):
    like = [(a.shape, a.dtype) for a in results]
    return pl.pallas_call(
        settle,
        out_shape=[jax.ShapeDtypeStruct(*a) for a in like],
        in_specs=[pl.BlockSpec(memory_space=pl.ANY)] * 5,
        out_specs=[pl.BlockSpec(memory_space=pl.ANY)] * 5,
        scratch_shapes=[*(pltpu.VMEM(*a) for a in like), DMA((5,)), DMA((5,))],
        name="settle",
    )(*results)


def body(patches, out_grad, conv_kernel, saved_gate, saved_up, w_gate, w_up, w_down):
    planes, height, breadth, features = patches.shape
    own = planes * height * breadth
    results = run(
        patches.reshape(own, features),
        out_grad.reshape(own, features),
        conv_kernel,
        saved_gate,
        saved_up,
        w_gate,
        w_up,
        w_down,
    )
    patch_grad, kernel_grad, gate_wgrad, up_wgrad, down_wgrad = run_settle(results)
    return (
        patch_grad.reshape(patches.shape),
        kernel_grad,
        gate_wgrad,
        up_wgrad,
        down_wgrad,
    )


def solution(mesh):
    return jax.shard_map(
        body,
        mesh=mesh,
        in_specs=(
            P("row", None, None, "col"),
            P("row", None, None, "col"),
            P(None, None, None, "col"),
            P("col", "row"),
            P("col", "row"),
            P("col", "row"),
            P("col", "row"),
            P("row", "col"),
        ),
        out_specs=(
            P("row", None, None, "col"),
            P(None, None, None, "col"),
            P("col", "row"),
            P("col", "row"),
            P("row", "col"),
        ),
        check_vma=False,
    )
```
